32 devices in a mesh: row: 8 (over z, core), col: 4 (over y, x).
Axes of the slice: x: 2, y: 2, z: 4, core: 2. Of those that a mesh axis runs over, the one named last changes fastest.
Arguments:
- amplitudes: float32 [16, 16, 160, 160], P('row', 'col'), may hold values from -8 to 8, as said below
- vvvv: float32 [160, 160, 160, 160], P('row', None, 'col'), may hold values from -0.0390625 to 0.0390625
- hole_ints: float32 [16, 16, 16, 16], replicated, may hold values from -0.375 to 0.375
- exchange_ints: float32 [16, 16, 160, 160], P('row', None, 'col'), may hold values from -0.0024414062 to 0.0024414062
- fock_occ: float32 [16, 16], replicated, may hold values from -1.5 to 1.5
- fock_vir: float32 [160, 160], replicated, may hold values from -0.5 to 0.5
- eps_occ: float32 [16], replicated, may hold values from -2 to -0.5
- eps_vir: float32 [160], replicated, may hold values from 0.3 to 3
Outputs:
- update: float32 [16, 16, 160, 160], P('row', 'col')
The draws below stay inside these ranges and needn't reach their ends.
Inputs may be any that keep to these rules, and one draw needn't show every extreme that they name: amplitudes[i, j, a, b] equals amplitudes[j, i, b, a].
All inputs are finite; a program needn't handle non-finite values.
Results may differ from the reference program's by a relative error of at most 0.000064.
Values sent between devices are 32-bit elements; how exact they have to be, the bound alone decides.
A program may use at most 256 MiB of HBM per device.

```python
import jax
import jax.numpy as jnp
from jax import lax

NO = 16
NV = 160


def draw_amplitudes(key, part):
    first_key = jax.random.fold_in(key, 11)
    initial = jax.random.normal(first_key, (NO, NO, NV, NV), jnp.float32)
    symmetric = (initial + initial.transpose(1, 0, 3, 2)) * 0.7071
    return jnp.clip(symmetric, -8.0, 8.0)


def shard_levels(key, dims, shards, least, high):
    loudness = 1.0
    for dim, blocks in shards:
        draws = jax.random.uniform(jax.random.fold_in(jax.random.fold_in(key, 6), dim), (blocks,), jnp.float32, least / len(shards), high / len(shards))
        loudness = loudness * jnp.repeat(jnp.exp(draws), dims[dim] // blocks).reshape((-1,) + (1,) * (len(dims) - 1 - dim))
    return loudness


def centred(stream_key, extent, scale, bound, pieces=(), dtype=jnp.bfloat16):
    gain = shard_levels(stream_key, extent, pieces, -0.22, 0.18) if pieces else 1.0
    array = jax.random.normal(stream_key, extent, jnp.float32) * scale * gain
    return jnp.minimum(jnp.maximum(array, -bound), bound).astype(dtype)


def setup_inputs(seed: int = 0) -> dict:
    keys = jax.random.split(jax.random.key(seed), 9)
    amplitudes = draw_amplitudes(jax.random.fold_in(keys[8], 71), 0)
    vvvv = centred(keys[1], (NV, NV, NV, NV), (NV * NV) ** -0.5, 0.0390625, ((0, 8), (2, 4)), jnp.float32)
    hole_ints = centred(keys[2], (NO, NO, NO, NO), (NO * NO) ** -0.5, 0.375, (), jnp.float32)
    exchange_ints = centred(keys[3], (NO, NO, NV, NV), (NO * NO * NV * NV) ** -0.5, 0.0024414062, ((0, 8), (2, 4)), jnp.float32)
    fock_occ = centred(keys[4], (NO, NO), NO ** -0.5, 1.5, (), jnp.float32)
    fock_vir = centred(keys[5], (NV, NV), NV ** -0.5, 0.5, (), jnp.float32)
    eps_occ = jnp.clip(jax.random.uniform(keys[6], (NO,), jnp.float32, -2.0, -0.5), -2.0, -0.5)
    eps_vir = jnp.clip(jax.random.uniform(keys[7], (NV,), jnp.float32, 0.3, 3.0), 0.3, 3.0)
    return {"amplitudes": amplitudes, "vvvv": vvvv, "hole_ints": hole_ints, "exchange_ints": exchange_ints, "fock_occ": fock_occ, "fock_vir": fock_vir, "eps_occ": eps_occ, "eps_vir": eps_vir}


def reference(amplitudes, vvvv, hole_ints, exchange_ints, fock_occ, fock_vir, eps_occ, eps_vir):
    highest = lax.Precision.HIGHEST
    matrix = amplitudes.reshape(NO * NO, NV * NV)
    ladder = lax.dot_general(matrix, vvvv.reshape(NV * NV, NV * NV), (((1,), (1,)), ((), ())), precision=highest)
    quadratic = lax.dot_general(matrix, exchange_ints.reshape(NO * NO, NV * NV), (((1,), (1,)), ((), ())), precision=highest)
    chi = hole_ints.reshape(NO * NO, NO * NO).T + quadratic
    hole = jnp.dot(chi, matrix, precision=highest)
    occupied_term = jnp.einsum("ikx,kj->ijx", amplitudes.reshape(NO, NO, NV * NV), fock_occ, precision=highest).reshape(NO * NO, NV * NV)
    raw = (ladder + hole - occupied_term).reshape(NO, NO, NV, NV)
    total = raw + raw.transpose(1, 0, 3, 2)
    total = total + jnp.einsum("ijac,cb->ijab", amplitudes, fock_vir, precision=highest)
    total = total + jnp.einsum("ac,ijcb->ijab", fock_vir, amplitudes, precision=highest)
    denominator = eps_occ[:, None, None, None] + eps_occ[None, :, None, None] - eps_vir[None, None, :, None] - eps_vir[None, None, None, :]
    return total / denominator
```

```python
import functools

import jax
import jax.numpy as jnp
from jax import lax
from jax.experimental import pallas as pl
from jax.experimental.pallas import tpu as pltpu
from jax.sharding import PartitionSpec as P

def finish(raw, amplitudes, fock_vir, eps_occ, eps_vir):
    high = lax.Precision.HIGH
    rows_n = lax.axis_size("row")
    cols_n = lax.axis_size("col")
    row = lax.axis_index("row")
    col = lax.axis_index("col")
    first_count, second_count, virtual = amplitudes.shape[:3]
    ratio = second_count // first_count
    others = []
    for turn in range(ratio):
        route = []
        for r in range(rows_n):
            for q in range(cols_n):
                m = (r + turn) % ratio
                route.append((r * cols_n + q, (q * ratio + m) * cols_n + r // ratio))
        m = lax.rem(row + turn, ratio)
        block = lax.dynamic_slice_in_dim(raw, m * first_count, first_count, axis=1)
        others.append(lax.ppermute(block, ("row", "col"), route))
    stacked = jnp.stack(others)
    order = jnp.stack([lax.rem(row - m + ratio, ratio) for m in range(ratio)])
    other = stacked[order].reshape(ratio, first_count, first_count, virtual, virtual)
    other = other.transpose(2, 0, 1, 4, 3)
    other = other.reshape(first_count, second_count, virtual, virtual)
    total = raw.reshape(first_count, second_count, virtual, virtual) + other
    total = total + jnp.einsum("ijac,cb->ijab", amplitudes, fock_vir, precision=high)
    total = total + jnp.einsum("ac,ijcb->ijab", fock_vir, amplitudes, precision=high)
    energy_rows = lax.dynamic_slice_in_dim(eps_occ, row * first_count, first_count)
    energy_cols = lax.dynamic_slice_in_dim(eps_occ, col * second_count, second_count)
    denominator = (
        energy_rows[:, None, None, None]
        + energy_cols[None, :, None, None]
        - eps_vir[None, None, :, None]
        - eps_vir[None, None, None, :]
    )
    return total / denominator


def plain(amplitudes, vvvv, hole_ints, exchange_ints, fock_occ, fock_vir, eps_occ, eps_vir):
    high = lax.Precision.HIGH
    rows_n = lax.axis_size("row")
    cols_n = lax.axis_size("col")
    row = lax.axis_index("row")
    col = lax.axis_index("col")
    first_count, second_count, virtual = amplitudes.shape[:3]
    occupied = fock_occ.shape[0]
    pairs_n = occupied * occupied
    a_count = vvvv.shape[0]
    c_count = vvvv.shape[2]
    k_count = exchange_ints.shape[0]

    split = lax.all_to_all(amplitudes, "col", split_axis=2, concat_axis=1, tiled=True)
    split = split.reshape(first_count * occupied, c_count * virtual)
    gathered = lax.all_gather(split, "row", axis=0, tiled=True)
    gathered = gathered.reshape(occupied, occupied, c_count, virtual)

    chi_part = lax.dot_general(
        gathered, exchange_ints, (((2, 3), (2, 3)), ((), ())), precision=high
    )
    chi_part = chi_part.reshape(pairs_n, k_count * occupied).T
    chi_all = lax.all_gather(chi_part, ("row", "col"), axis=0)
    chi = chi_all.reshape(rows_n, cols_n, k_count * occupied, pairs_n).sum(axis=1)
    delta = jnp.eye(occupied, dtype=fock_occ.dtype)
    known = hole_ints - delta[:, None, :, None] * fock_occ[None, :, None, :]
    mixing = chi.reshape(pairs_n, pairs_n) + known.reshape(pairs_n, pairs_n)

    mine = lax.dynamic_slice_in_dim(gathered, row * a_count, a_count, axis=3)
    mine = mine.transpose(1, 0, 3, 2).reshape(pairs_n, a_count * c_count)
    placed = lax.all_gather(mine, "col", axis=0)
    placed = placed.reshape(cols_n, pairs_n, a_count, c_count).transpose(1, 2, 0, 3)
    placed = placed.reshape(pairs_n, a_count * virtual)

    part = lax.dot_general(gathered, vvvv, (((2, 3), (2, 3)), ((), ())), precision=high)
    part = part.transpose(1, 0, 2, 3).reshape(occupied, occupied, a_count * virtual)
    raw = lax.psum_scatter(part, "col", scatter_dimension=0, tiled=True)
    chosen = lax.dynamic_slice_in_dim(
        mixing.reshape(pairs_n, occupied, occupied), col * second_count, second_count, axis=2
    )
    chosen = chosen.transpose(0, 2, 1).reshape(pairs_n, second_count * occupied)
    hole = lax.dot_general(chosen, placed, (((0,), (0,)), ((), ())), precision=high)
    raw = raw + hole.reshape(raw.shape)
    raw = raw.reshape(second_count, rows_n, first_count, a_count * virtual)
    raw = raw.transpose(1, 2, 0, 3)
    raw = lax.all_to_all(raw, "row", split_axis=0, concat_axis=0, tiled=True)
    raw = raw.transpose(1, 2, 0, 3).reshape(first_count, second_count, virtual * virtual)

    return finish(raw, amplitudes, fock_vir, eps_occ, eps_vir)


F32 = jnp.float32
BF16 = jnp.bfloat16


def split(x):
    high = x.astype(BF16)
    return high, (x - high.astype(F32)).astype(BF16)


def product(a, b, dims):
    return lax.dot_general(a, b, (dims, ((), ())), preferred_element_type=F32)


def contract_kernel(take, slots, flip, v_ref, t_ref, o_ref, buf, rest, spread, high, low, acc, w_high, w_low, sem):
    a_count, b_count, c_count, virtual = v_ref.shape
    group = buf.shape[4 - 1]
    lanes = buf.shape[4]
    tail = virtual - lanes
    rows = take * b_count
    chunks = c_count // group
    blocks = a_count // take
    steps = chunks * blocks
    per = lanes // tail
    width = t_ref.shape[-1]

    def copies(step):
        slot = lax.rem(step, slots)
        chunk, block = step // blocks, lax.rem(step, blocks)
        source = v_ref.at[
            pl.ds(block * take, take), :, pl.ds(pl.multiple_of(chunk * group, group), group), :
        ]
        return (
            pltpu.make_async_copy(source.at[:, :, :, pl.ds(0, lanes)], buf.at[slot], sem.at[slot, 0]),
            pltpu.make_async_copy(source.at[:, :, :, pl.ds(lanes, tail)], rest.at[slot], sem.at[slot, 1]),
        )

    for step in range(min(slots - 1, steps)):
        for copy in copies(step):
            copy.start()
    acc[...] = jnp.zeros_like(acc)
    lane = lax.broadcasted_iota(jnp.int32, (rows, lanes), 1)

    def body(step, _):
        slot = lax.rem(step, slots)
        chunk, block = step // blocks, lax.rem(step, blocks)
        for copy in copies(step):
            copy.wait()

        @pl.when(step + slots - 1 < steps)
        def _():
            for copy in copies(step + slots - 1):
                copy.start()

        @pl.when(block == 0)
        def _():
            for r in range(t_ref.shape[0]):
                for q in range(t_ref.shape[1]):
                    n = t_ref.shape[3]
                    at = (r * t_ref.shape[1] + q) * n
                    hi, lo = split(t_ref[r, q, chunk])
                    w_high[at : at + n, :] = hi
                    w_low[at : at + n, :] = lo

        main = buf.at[slot].reshape(rows * group, lanes)
        spread[:, pl.ds(0, tail)] = rest.at[slot].reshape(rows * group, tail)[...]
        packed = None
        for c in range(group):
            hi, lo = split(main[pl.ds(c, rows, stride=group), :])
            high[:, c * lanes : (c + 1) * lanes] = hi
            low[:, c * lanes : (c + 1) * lanes] = lo
            piece = spread[pl.ds(c, rows, stride=group), :]
            k = c % per
            packed = piece if k == 0 else jnp.where(lane < tail * k, packed, pltpu.roll(piece, tail * k, 1))
            if k == per - 1:
                at = (group + c // per) * lanes
                hi, lo = split(packed)
                high[:, at : at + lanes] = hi
                low[:, at : at + lanes] = lo
        dims = ((1,), (1,))
        acc[block] += (
            product(high[...], w_high[...], dims)
            + product(low[...], w_high[...], dims)
            + product(high[...], w_low[...], dims)
        )
        return 0

    lax.fori_loop(0, steps, body, 0)
    if not flip:
        o_ref[...] = acc[0]
        return
    rows_n, cols_n, _, n, _ = t_ref.shape
    for block in range(blocks):
        turned = acc[block].T
        for r in range(rows_n):
            for q in range(cols_n):
                at = (r * cols_n + q) * n
                o_ref[q, r * n : (r + 1) * n, block * rows : (block + 1) * rows] = turned[at : at + n, :]


def contract(v, t, take, slots, flip):
    a_count, b_count, c_count, virtual = v.shape
    rows_n, cols_n, chunks, n, width = t.shape
    pairs = rows_n * cols_n * n
    group, lanes = c_count // chunks, 128
    rows = take * b_count
    shape = (cols_n, rows_n * n, a_count * b_count) if flip else (rows, pairs)
    return pl.pallas_call(
        functools.partial(contract_kernel, take, slots, flip),
        out_shape=jax.ShapeDtypeStruct(shape, F32),
        in_specs=[pl.BlockSpec(memory_space=pl.ANY), pl.BlockSpec(memory_space=pltpu.VMEM)],
        out_specs=pl.BlockSpec(memory_space=pltpu.VMEM),
        scratch_shapes=[
            pltpu.VMEM((slots, take, b_count, group, lanes), F32),
            pltpu.VMEM((slots, take, b_count, group, virtual - lanes), F32),
            pltpu.VMEM((rows * group, lanes), F32),
            pltpu.VMEM((rows, width), BF16),
            pltpu.VMEM((rows, width), BF16),
            pltpu.VMEM((a_count // take, rows, pairs), F32),
            pltpu.VMEM((pairs, width), BF16),
            pltpu.VMEM((pairs, width), BF16),
            pltpu.SemaphoreType.DMA((slots, 2)),
        ],
        compiler_params=pltpu.CompilerParams(vmem_limit_bytes=60 << 20),
        cost_estimate=pl.CostEstimate(
            flops=6 * v.size * pairs, bytes_accessed=4 * v.size, transcendentals=0
        ),
    )(v, t)


def fast(amplitudes, vvvv, hole_ints, exchange_ints, fock_occ, fock_vir, eps_occ, eps_vir):
    high = lax.Precision.HIGH
    rows_n = lax.axis_size("row")
    cols_n = lax.axis_size("col")
    row = lax.axis_index("row")
    col = lax.axis_index("col")
    first, second, virtual = amplitudes.shape[:3]
    occupied = fock_occ.shape[0]
    pairs = occupied * occupied
    a_count, c_count = vvvv.shape[0], vvvv.shape[2]
    group, lanes = 8, 128
    tail = virtual - lanes
    chunks = c_count // group
    n = first * second

    x = amplitudes.reshape(n, cols_n, chunks, group, virtual)
    x = jnp.concatenate(
        [
            x[..., :lanes].reshape(n, cols_n, chunks, group * lanes),
            x[..., lanes:].reshape(n, cols_n, chunks, group * tail),
        ],
        axis=-1,
    ).transpose(1, 2, 0, 3)
    x = lax.all_to_all(x, "col", split_axis=0, concat_axis=0, tiled=True)
    t = lax.all_gather(x, "row", axis=0)

    chi_part = contract(exchange_ints, t, exchange_ints.shape[0], 3, False)
    chi_all = lax.all_gather(chi_part, ("row", "col"), axis=0)
    chi = chi_all.reshape(rows_n, cols_n, -1, pairs).sum(axis=1).reshape(pairs, pairs)
    delta = jnp.eye(occupied, dtype=fock_occ.dtype)
    known = hole_ints - delta[:, None, :, None] * fock_occ[None, :, None, :]
    known = known.reshape(pairs, rows_n, first, cols_n, second).transpose(0, 3, 1, 2, 4)

    part = contract(vvvv, t, 4, 3, True)

    chi = chi.reshape(pairs, rows_n, cols_n, first, second).transpose(0, 2, 1, 3, 4)
    mixing = (chi + known).reshape(occupied, occupied, pairs)
    wide = t.reshape(rows_n, cols_n, chunks, n, -1)
    main = wide[..., : group * lanes].reshape(rows_n, cols_n, chunks, n, group, lanes)
    rest = wide[..., group * lanes :].reshape(rows_n, cols_n, chunks, n, group, tail)
    whole = jnp.concatenate([main, rest], axis=-1)
    mine = lax.dynamic_slice_in_dim(whole, row * a_count, a_count, axis=5)
    mine = mine.reshape(rows_n, cols_n, chunks, first, second, group, a_count)
    mine = mine.transpose(1, 4, 0, 3, 6, 2, 5).reshape(pairs, a_count * c_count)
    hole = lax.dot_general(
        mixing.reshape(pairs, pairs), mine, (((0,), (0,)), ((), ())), precision=high
    )
    hole = hole.reshape(cols_n, rows_n * n, a_count, c_count)
    part = part.reshape(cols_n, rows_n * n, a_count, virtual)
    spot = lax.dynamic_slice_in_dim(part, col * c_count, c_count, axis=3) + hole
    part = lax.dynamic_update_slice_in_dim(part, spot, col * c_count, axis=3)
    part = part.reshape(cols_n, rows_n * n, a_count * virtual)
    raw = lax.psum_scatter(part, "col", scatter_dimension=0, tiled=False)
    raw = raw.reshape(rows_n, n, a_count * virtual)
    raw = lax.all_to_all(raw, "row", split_axis=0, concat_axis=0, tiled=True)
    raw = raw.transpose(1, 0, 2).reshape(first, second, virtual * virtual)
    return finish(raw, amplitudes, fock_vir, eps_occ, eps_vir)


def on_device(amplitudes, vvvv, *rest):
    virtual, b_count, c_count = amplitudes.shape[2], vvvv.shape[1], vvvv.shape[2]
    tail = virtual - 128
    fits = (
        virtual > 128
        and 128 % tail == 0
        and c_count % 8 == 0
        and (8 * tail) % 128 == 0
        and vvvv.shape[0] % 4 == 0
        and (4 * b_count) % 128 == 0
        and (amplitudes.shape[0] * amplitudes.shape[1]) % 8 == 0
    )
    return (fast if fits else plain)(amplitudes, vvvv, *rest)


def solution(mesh):
    in_specs = (
        P("row", "col", None, None),
        P("row", None, "col", None),
        P(),
        P("row", None, "col", None),
        P(),
        P(),
        P(),
        P(),
    )
    out_specs = P("row", "col", None, None)
    return jax.shard_map(
        on_device, mesh=mesh, in_specs=in_specs, out_specs=out_specs, check_vma=False
    )
```

```python
import functools

import jax
import jax.numpy as jnp
from jax import lax
from jax.experimental import pallas as pl
from jax.experimental.pallas import tpu as pltpu
from jax.sharding import PartitionSpec as P

def finish(raw, amplitudes, fock_vir, eps_occ, eps_vir):
    high = lax.Precision.HIGH
    rows_n = lax.axis_size("row")
    cols_n = lax.axis_size("col")
    row = lax.axis_index("row")
    col = lax.axis_index("col")
    first_count, second_count, virtual = amplitudes.shape[:3]
    ratio = second_count // first_count
    others = []
    for turn in range(ratio):
        route = []
        for r in range(rows_n):
            for q in range(cols_n):
                m = (r + turn) % ratio
                route.append((r * cols_n + q, (q * ratio + m) * cols_n + r // ratio))
        m = lax.rem(row + turn, ratio)
        block = lax.dynamic_slice_in_dim(raw, m * first_count, first_count, axis=1)
        others.append(lax.ppermute(block, ("row", "col"), route))
    stacked = jnp.stack(others)
    order = jnp.stack([lax.rem(row - m + ratio, ratio) for m in range(ratio)])
    other = stacked[order].reshape(ratio, first_count, first_count, virtual, virtual)
    other = other.transpose(2, 0, 1, 4, 3)
    other = other.reshape(first_count, second_count, virtual, virtual)
    total = raw.reshape(first_count, second_count, virtual, virtual) + other
    return close(total, amplitudes, fock_vir, eps_occ, eps_vir)


def close(total, amplitudes, fock_vir, eps_occ, eps_vir):
    high = lax.Precision.HIGH
    row = lax.axis_index("row")
    col = lax.axis_index("col")
    first_count, second_count = amplitudes.shape[:2]
    total = total + jnp.einsum("ijac,cb->ijab", amplitudes, fock_vir, precision=high)
    total = total + jnp.einsum("ac,ijcb->ijab", fock_vir, amplitudes, precision=high)
    energy_rows = lax.dynamic_slice_in_dim(eps_occ, row * first_count, first_count)
    energy_cols = lax.dynamic_slice_in_dim(eps_occ, col * second_count, second_count)
    denominator = (
        energy_rows[:, None, None, None]
        + energy_cols[None, :, None, None]
        - eps_vir[None, None, :, None]
        - eps_vir[None, None, None, :]
    )
    return total / denominator


def plain(amplitudes, vvvv, hole_ints, exchange_ints, fock_occ, fock_vir, eps_occ, eps_vir):
    high = lax.Precision.HIGH
    rows_n = lax.axis_size("row")
    cols_n = lax.axis_size("col")
    row = lax.axis_index("row")
    col = lax.axis_index("col")
    first_count, second_count, virtual = amplitudes.shape[:3]
    occupied = fock_occ.shape[0]
    pairs_n = occupied * occupied
    a_count = vvvv.shape[0]
    c_count = vvvv.shape[2]
    k_count = exchange_ints.shape[0]

    split = lax.all_to_all(amplitudes, "col", split_axis=2, concat_axis=1, tiled=True)
    split = split.reshape(first_count * occupied, c_count * virtual)
    gathered = lax.all_gather(split, "row", axis=0, tiled=True)
    gathered = gathered.reshape(occupied, occupied, c_count, virtual)

    chi_part = lax.dot_general(
        gathered, exchange_ints, (((2, 3), (2, 3)), ((), ())), precision=high
    )
    chi_part = chi_part.reshape(pairs_n, k_count * occupied).T
    chi_all = lax.all_gather(chi_part, ("row", "col"), axis=0)
    chi = chi_all.reshape(rows_n, cols_n, k_count * occupied, pairs_n).sum(axis=1)
    delta = jnp.eye(occupied, dtype=fock_occ.dtype)
    known = hole_ints - delta[:, None, :, None] * fock_occ[None, :, None, :]
    mixing = chi.reshape(pairs_n, pairs_n) + known.reshape(pairs_n, pairs_n)

    mine = lax.dynamic_slice_in_dim(gathered, row * a_count, a_count, axis=3)
    mine = mine.transpose(1, 0, 3, 2).reshape(pairs_n, a_count * c_count)
    placed = lax.all_gather(mine, "col", axis=0)
    placed = placed.reshape(cols_n, pairs_n, a_count, c_count).transpose(1, 2, 0, 3)
    placed = placed.reshape(pairs_n, a_count * virtual)

    part = lax.dot_general(gathered, vvvv, (((2, 3), (2, 3)), ((), ())), precision=high)
    part = part.transpose(1, 0, 2, 3).reshape(occupied, occupied, a_count * virtual)
    raw = lax.psum_scatter(part, "col", scatter_dimension=0, tiled=True)
    chosen = lax.dynamic_slice_in_dim(
        mixing.reshape(pairs_n, occupied, occupied), col * second_count, second_count, axis=2
    )
    chosen = chosen.transpose(0, 2, 1).reshape(pairs_n, second_count * occupied)
    hole = lax.dot_general(chosen, placed, (((0,), (0,)), ((), ())), precision=high)
    raw = raw + hole.reshape(raw.shape)
    raw = raw.reshape(second_count, rows_n, first_count, a_count * virtual)
    raw = raw.transpose(1, 2, 0, 3)
    raw = lax.all_to_all(raw, "row", split_axis=0, concat_axis=0, tiled=True)
    raw = raw.transpose(1, 2, 0, 3).reshape(first_count, second_count, virtual * virtual)

    return finish(raw, amplitudes, fock_vir, eps_occ, eps_vir)


F32 = jnp.float32
BF16 = jnp.bfloat16


def split(x):
    high = x.astype(BF16)
    return high, (x - high.astype(F32)).astype(BF16)


def product(a, b, dims):
    return lax.dot_general(a, b, (dims, ((), ())), preferred_element_type=F32)


def contract_kernel(take, slots, v_ref, t_ref, o_ref, buf, rest, spread, high, low, acc, w_high, w_low, sem):
    a_count, b_count, c_count, virtual = v_ref.shape
    group = buf.shape[4 - 1]
    lanes = buf.shape[4]
    tail = virtual - lanes
    rows = take * b_count
    chunks = c_count // group
    blocks = a_count // take
    steps = chunks * blocks
    per = lanes // tail
    width = t_ref.shape[-1]

    def copies(step):
        slot = lax.rem(step, slots)
        chunk, block = step // blocks, lax.rem(step, blocks)
        source = v_ref.at[
            pl.ds(block * take, take), :, pl.ds(pl.multiple_of(chunk * group, group), group), :
        ]
        return (
            pltpu.make_async_copy(source.at[:, :, :, pl.ds(0, lanes)], buf.at[slot], sem.at[slot, 0]),
            pltpu.make_async_copy(source.at[:, :, :, pl.ds(lanes, tail)], rest.at[slot], sem.at[slot, 1]),
        )

    for step in range(min(slots - 1, steps)):
        for copy in copies(step):
            copy.start()
    acc[...] = jnp.zeros_like(acc)
    lane = lax.broadcasted_iota(jnp.int32, (rows, lanes), 1)

    def body(step, _):
        slot = lax.rem(step, slots)
        chunk, block = step // blocks, lax.rem(step, blocks)
        for copy in copies(step):
            copy.wait()

        @pl.when(step + slots - 1 < steps)
        def _():
            for copy in copies(step + slots - 1):
                copy.start()

        @pl.when(block == 0)
        def _():
            for r in range(t_ref.shape[0]):
                for q in range(t_ref.shape[2]):
                    n = t_ref.shape[3]
                    at = (r * t_ref.shape[2] + q) * n
                    hi, lo = split(t_ref[r, chunk, q])
                    w_high[at : at + n, :] = hi
                    w_low[at : at + n, :] = lo

        main = buf.at[slot].reshape(rows * group, lanes)
        spread[:, pl.ds(0, tail)] = rest.at[slot].reshape(rows * group, tail)[...]
        packed = None
        for c in range(group):
            hi, lo = split(main[pl.ds(c, rows, stride=group), :])
            high[:, c * lanes : (c + 1) * lanes] = hi
            low[:, c * lanes : (c + 1) * lanes] = lo
            piece = spread[pl.ds(c, rows, stride=group), :]
            k = c % per
            packed = piece if k == 0 else jnp.where(lane < tail * k, packed, pltpu.roll(piece, tail * k, 1))
            if k == per - 1:
                at = (group + c // per) * lanes
                hi, lo = split(packed)
                high[:, at : at + lanes] = hi
                low[:, at : at + lanes] = lo
        dims = ((1,), (1,))
        acc[block] += (
            product(high[...], w_high[...], dims)
            + product(low[...], w_high[...], dims)
            + product(high[...], w_low[...], dims)
        )
        return 0

    lax.fori_loop(0, steps, body, 0)
    for block in range(blocks):
        o_ref[block * rows : (block + 1) * rows, :] = acc[block]


def contract(v, t, take, slots):
    a_count, b_count, c_count, virtual = v.shape
    rows_n, chunks, cols_n, n, width = t.shape
    pairs = rows_n * cols_n * n
    group, lanes = c_count // chunks, 128
    rows = take * b_count
    shape = (a_count * b_count, pairs)
    return pl.pallas_call(
        functools.partial(contract_kernel, take, slots),
        out_shape=jax.ShapeDtypeStruct(shape, F32),
        in_specs=[pl.BlockSpec(memory_space=pl.ANY), pl.BlockSpec(memory_space=pltpu.VMEM)],
        out_specs=pl.BlockSpec(memory_space=pltpu.VMEM),
        scratch_shapes=[
            pltpu.VMEM((slots, take, b_count, group, lanes), F32),
            pltpu.VMEM((slots, take, b_count, group, virtual - lanes), F32),
            pltpu.VMEM((rows * group, lanes), F32),
            pltpu.VMEM((rows, width), BF16),
            pltpu.VMEM((rows, width), BF16),
            pltpu.VMEM((a_count // take, rows, pairs), F32),
            pltpu.VMEM((pairs, width), BF16),
            pltpu.VMEM((pairs, width), BF16),
            pltpu.SemaphoreType.DMA((slots, 2)),
        ],
        compiler_params=pltpu.CompilerParams(vmem_limit_bytes=60 << 20),
        cost_estimate=pl.CostEstimate(
            flops=6 * v.size * pairs, bytes_accessed=4 * v.size, transcendentals=0
        ),
    )(v, t)


def hole_kernel(a_count, c_count, virtual, part_ref, t_ref, mixing_ref, o_ref, w_high, w_low, picked, add):
    rows_n, chunks, cols_n, n, width = t_ref.shape
    pairs = rows_n * cols_n * n
    lanes = 128
    tail = virtual - lanes
    group = c_count // chunks
    per = lanes // tail
    b_count = part_ref.shape[0] // a_count
    row, col = lax.axis_index("row"), lax.axis_index("col")
    up = -(-a_count // 16) * 16
    spot = row * a_count + lax.broadcasted_iota(jnp.int32, (up, lanes), 0)
    lane = lax.broadcasted_iota(jnp.int32, (up, lanes), 1)
    first = jnp.where(spot == lane, 1.0, 0.0).astype(BF16)
    later = [jnp.where(spot - lanes == lane - k * tail, 1.0, 0.0) for k in range(per)]
    later = [
        jnp.where((lane >= k * tail) & (lane < (k + 1) * tail), later[k], 0.0).astype(BF16)
        for k in range(per)
    ]
    dims = ((1,), (1,))
    for chunk in range(chunks):
        for r in range(rows_n):
            for q in range(cols_n):
                at = (r * cols_n + q) * n
                hi, lo = split(t_ref[r, chunk, q])
                w_high[at : at + n, :] = hi
                w_low[at : at + n, :] = lo
        for c in range(group):
            at = (group + c // per) * lanes
            k = c % per
            total = None
            for w in (w_high, w_low):
                value = product(first, w[:, c * lanes : (c + 1) * lanes], dims)
                value += product(later[k], w[:, at : at + lanes], dims)
                total = value if total is None else total + value
            for half in range(pairs // lanes):
                picked[half, pl.ds(chunk * group + c, a_count, stride=c_count), :] = total[
                    :a_count, half * lanes : (half + 1) * lanes
                ]
    mix_high, mix_low = split(mixing_ref[...])
    total = None
    for half in range(pairs // lanes):
        hi, lo = split(picked[half])
        at = slice(half * lanes, (half + 1) * lanes)
        value = (
            product(hi, mix_high[at, :], ((1,), (0,)))
            + product(lo, mix_high[at, :], ((1,), (0,)))
            + product(hi, mix_low[at, :], ((1,), (0,)))
        )
        total = value if total is None else total + value
    add[...] = part_ref[...]
    for a in range(a_count):
        at = pl.ds(pl.multiple_of(a * b_count + col * c_count, 8), c_count)
        add[at, :] += total[a * c_count : (a + 1) * c_count, :]
    step = 5 * lanes
    for block in range(part_ref.shape[0] // step):
        turned = add[block * step : (block + 1) * step, :].T
        for r in range(rows_n):
            for q in range(cols_n):
                at = (r * cols_n + q) * n
                for h in range(2):
                    o_ref[q, r, h, :, block * step : (block + 1) * step] = turned[
                        at + h * n // 2 : at + (h + 1) * n // 2, :
                    ]


def hole(part, t, mixing, a_count, c_count, virtual):
    rows_n, chunks, cols_n, n, width = t.shape
    pairs = rows_n * cols_n * n
    return pl.pallas_call(
        functools.partial(hole_kernel, a_count, c_count, virtual),
        out_shape=jax.ShapeDtypeStruct((cols_n, rows_n, 2, n // 2, part.shape[0]), F32),
        in_specs=[pl.BlockSpec(memory_space=pltpu.VMEM)] * 3,
        out_specs=pl.BlockSpec(memory_space=pltpu.VMEM),
        scratch_shapes=[
            pltpu.VMEM((pairs, width), BF16),
            pltpu.VMEM((pairs, width), BF16),
            pltpu.VMEM((pairs // 128, a_count * c_count, 128), F32),
            pltpu.VMEM(part.shape, F32),
        ],
        compiler_params=pltpu.CompilerParams(vmem_limit_bytes=60 << 20),
    )(part, t, mixing)


def exchange_kernel(
    part_ref, straight_ref, turned_ref, got, last, onward, sums, middle,
    send_a, recv_a, send_b, recv_b, send_c, recv_c, send_d, recv_d, send_e, recv_e, own,
):
    cols_n, rows_n = part_ref.shape[:2]
    row, col = lax.axis_index("row"), lax.axis_index("col")
    flips = (col + 1 - 2 * (col % 2), (col + 2) % 4)
    far = 3 - col

    def remote(source, target, send, recv, r, q):
        return pltpu.make_async_remote_copy(
            src_ref=source, dst_ref=target, send_sem=send, recv_sem=recv,
            device_id=(r, q), device_id_type=pl.DeviceIdType.MESH,
        )

    barrier = pltpu.get_barrier_semaphore()
    for q in (flips[0], flips[1], far):
        pl.semaphore_signal(barrier, inc=1, device_id=(row, q), device_id_type=pl.DeviceIdType.MESH)
    for k in range(1, rows_n):
        r = (row + k) % rows_n
        pl.semaphore_signal(barrier, inc=1, device_id=(r, col), device_id_type=pl.DeviceIdType.MESH)
    pl.semaphore_wait(barrier, cols_n - 1 + rows_n - 1)

    def pair(k):
        return flips if k < rows_n // 2 else (flips[1], flips[0])

    def scatter(k):
        near = pair(k)[0]
        return [
            remote(part_ref.at[near, k], got.at[k, 0], send_a.at[k, 0], recv_a.at[k, 0], row, near),
            remote(part_ref.at[far, k], got.at[k, 1], send_a.at[k, 1], recv_a.at[k, 1], row, near),
        ]

    def pass_on(k):
        return remote(onward.at[k], last.at[k], send_b.at[k], recv_b.at[k], row, pair(k)[1])

    def deliver(k):
        return remote(sums.at[k], straight_ref.at[row], send_c.at[k], recv_c.at[row], k, col)

    def deliver_own(k):
        return pltpu.make_async_copy(sums.at[k], straight_ref.at[row], own.at[0])

    def cross(k):
        return remote(sums.at[k], middle.at[k % 2, col], send_d.at[k], recv_d.at[k % 2, col], row, k // 2)

    def cross_own(k):
        return pltpu.make_async_copy(sums.at[k], middle.at[k % 2, col], own.at[1 + k % 2])

    def spread(m, q, h):
        return remote(
            middle.at[m, q, h], turned_ref.at[row, m], send_e.at[m, q, h], recv_e.at[row, m], 2 * q + h, col
        )

    def spread_own(m, q, h):
        return pltpu.make_async_copy(middle.at[m, q, h], turned_ref.at[row, m], own.at[3 + m])

    order = [k for m in range(rows_n // 2) for k in (m, rows_n // 2 + m)]
    ahead = 4
    for k in order[:ahead]:
        for copy in scatter(k):
            copy.start()

    def first(k):
        for copy in scatter(k):
            copy.wait_recv()
        onward[k] = part_ref[pair(k)[1], k] + got[k, 1]
        sums[k] = part_ref[col, k] + got[k, 0]
        pass_on(k).start()

    def second(k):
        pass_on(k).wait_recv()
        sums[k] = sums[k] + last[k]

        @pl.when(row != k)
        def _():
            deliver(k).start()

        @pl.when(row == k)
        def _():
            deliver_own(k).start()

        @pl.when(col != k // 2)
        def _():
            cross(k).start()

        @pl.when(col == k // 2)
        def _():
            cross_own(k).start()

    for at, k in enumerate(order):
        if at + ahead < rows_n:
            for copy in scatter(order[at + ahead]):
                copy.start()
        first(k)
        if at >= 2:
            second(order[at - 2])
    for k in order[-2:]:
        second(k)

    def arrived(m, q):
        @pl.when(col != q)
        def _():
            remote(sums.at[0], middle.at[m, q], send_d.at[0], recv_d.at[m, q], row, q).wait_recv()

    for m in range(2):
        for k in range(cols_n):
            @pl.when(col == k)
            def _():
                cross_own(2 * k + m).wait()
    for m in range(2):
        for q in range(cols_n):
            arrived(m, q)
            for h in range(2):
                @pl.when(row != 2 * q + h)
                def _():
                    spread(m, q, h).start()

                @pl.when(row == 2 * q + h)
                def _():
                    spread_own(m, q, h).start()
    for k in range(rows_n):
        for copy in scatter(k):
            copy.wait_send()
        pass_on(k).wait_send()

        @pl.when(row != k)
        def _():
            deliver(k).wait_send()
            remote(sums.at[0], straight_ref.at[k], send_c.at[k], recv_c.at[k], k, col).wait_recv()
            for m in range(2):
                spread(m, k // 2, k % 2).wait_send()
                remote(
                    middle.at[m, 0, 0], turned_ref.at[k, m], send_e.at[m, 0, 0], recv_e.at[k, m], k, col
                ).wait_recv()

        @pl.when(row == k)
        def _():
            deliver_own(k).wait()
            for m in range(2):
                spread_own(m, k // 2, k % 2).wait()

        @pl.when(col != k // 2)
        def _():
            cross(k).wait_send()


def exchange(part):
    cols_n, rows_n, _, n, width = part.shape
    block = (2, n, width)
    dma = pltpu.SemaphoreType.DMA
    return pl.pallas_call(
        exchange_kernel,
        out_shape=[jax.ShapeDtypeStruct((rows_n,) + block, F32)] * 2,
        in_specs=[pl.BlockSpec(memory_space=pltpu.VMEM)],
        out_specs=[pl.BlockSpec(memory_space=pltpu.VMEM)] * 2,
        scratch_shapes=[
            pltpu.VMEM((rows_n, 2) + block, F32),
            pltpu.VMEM((rows_n,) + block, F32),
            pltpu.VMEM((rows_n,) + block, F32),
            pltpu.VMEM((rows_n,) + block, F32),
            pltpu.VMEM((2, cols_n) + block, F32),
            dma((rows_n, 2)), dma((rows_n, 2)),
            dma((rows_n,)), dma((rows_n,)),
            dma((rows_n,)), dma((rows_n,)),
            dma((rows_n,)), dma((2, cols_n)),
            dma((2, cols_n, 2)), dma((rows_n, 2)),
            dma((5,)),
        ],
        compiler_params=pltpu.CompilerParams(
            collective_id=1, has_side_effects=True, vmem_limit_bytes=40 << 20
        ),
    )(part)


def fast(amplitudes, vvvv, hole_ints, exchange_ints, fock_occ, fock_vir, eps_occ, eps_vir):
    high = lax.Precision.HIGH
    rows_n = lax.axis_size("row")
    cols_n = lax.axis_size("col")
    row = lax.axis_index("row")
    col = lax.axis_index("col")
    first, second, virtual = amplitudes.shape[:3]
    occupied = fock_occ.shape[0]
    pairs = occupied * occupied
    a_count, c_count = vvvv.shape[0], vvvv.shape[2]
    group, lanes = 8, 128
    tail = virtual - lanes
    chunks = c_count // group
    n = first * second

    half = second // 2
    x = amplitudes.reshape(first, 2, half, virtual, virtual).transpose(1, 0, 2, 3, 4)
    x = x.reshape(n, cols_n, chunks, group, virtual)
    x = jnp.concatenate(
        [
            x[..., :lanes].reshape(n, cols_n, chunks, group * lanes),
            x[..., lanes:].reshape(n, cols_n, chunks, group * tail),
        ],
        axis=-1,
    ).transpose(1, 2, 0, 3)
    x = lax.all_to_all(x, "col", split_axis=0, concat_axis=0, tiled=True)
    t = lax.all_gather(x.transpose(1, 0, 2, 3), "row", axis=0)

    chi_part = contract(exchange_ints, t, exchange_ints.shape[0], 3)
    chi_all = lax.all_gather(chi_part, ("row", "col"), axis=0)
    chi = chi_all.reshape(rows_n, cols_n, -1, pairs).sum(axis=1).reshape(pairs, pairs)
    delta = jnp.eye(occupied, dtype=fock_occ.dtype)
    known = hole_ints - delta[:, None, :, None] * fock_occ[None, :, None, :]
    highest = lax.Precision.HIGHEST
    one, two = jnp.divmod(jnp.arange(pairs, dtype=jnp.int32), occupied)

    def place(i, j):
        inner = (j % second) // half * (first * half) + (i % first) * half + j % half
        return ((i // first) * cols_n + j // second) * n + inner

    spots = jnp.arange(pairs, dtype=jnp.int32)
    turn = (place(one, two)[:, None] == spots[None, :]).astype(F32)
    move = (spots[:, None] == place(two, one)[None, :]).astype(F32)
    known = jnp.dot(known.reshape(pairs, pairs), turn, precision=highest)

    part = contract(vvvv, t, 4, 3)

    mixing = jnp.dot(move, chi + known, precision=highest)
    part = hole(part, t, mixing, a_count, c_count, virtual)
    straight, turned = exchange(part)
    straight = straight.reshape(rows_n, 2, first, half, a_count, virtual)
    straight = straight.transpose(2, 1, 3, 0, 4, 5).reshape(first, second, virtual, virtual)
    turned = turned.reshape(rows_n, 2, half, first, a_count, virtual)
    turned = turned.transpose(3, 1, 2, 5, 0, 4).reshape(first, second, virtual, virtual)
    return close(straight + turned, amplitudes, fock_vir, eps_occ, eps_vir)


def on_device(amplitudes, vvvv, *rest):
    virtual, b_count, c_count = amplitudes.shape[2], vvvv.shape[1], vvvv.shape[2]
    tail = virtual - 128
    fits = (
        virtual > 128
        and 128 % tail == 0
        and c_count % 8 == 0
        and (8 * tail) % 128 == 0
        and vvvv.shape[0] % 4 == 0
        and (4 * b_count) % 128 == 0
        and (amplitudes.shape[0] * amplitudes.shape[1]) % 8 == 0
        and amplitudes.shape[1] == 2 * amplitudes.shape[0]
        and lax.axis_size("row") == 2 * lax.axis_size("col")
        and lax.axis_size("col") == 4
    )
    return (fast if fits else plain)(amplitudes, vvvv, *rest)


def solution(mesh):
    in_specs = (
        P("row", "col", None, None),
        P("row", None, "col", None),
        P(),
        P("row", None, "col", None),
        P(),
        P(),
        P(),
        P(),
    )
    out_specs = P("row", "col", None, None)
    return jax.shard_map(
        on_device, mesh=mesh, in_specs=in_specs, out_specs=out_specs, check_vma=False
    )
```

```python
import functools

import jax
import jax.numpy as jnp
from jax import lax
from jax.experimental import pallas as pl
from jax.experimental.pallas import tpu as pltpu
from jax.sharding import PartitionSpec as P

def finish(raw, amplitudes, fock_vir, eps_occ, eps_vir):
    high = lax.Precision.HIGH
    rows_n = lax.axis_size("row")
    cols_n = lax.axis_size("col")
    row = lax.axis_index("row")
    col = lax.axis_index("col")
    first_count, second_count, virtual = amplitudes.shape[:3]
    ratio = second_count // first_count
    others = []
    for turn in range(ratio):
        route = []
        for r in range(rows_n):
            for q in range(cols_n):
                m = (r + turn) % ratio
                route.append((r * cols_n + q, (q * ratio + m) * cols_n + r // ratio))
        m = lax.rem(row + turn, ratio)
        block = lax.dynamic_slice_in_dim(raw, m * first_count, first_count, axis=1)
        others.append(lax.ppermute(block, ("row", "col"), route))
    stacked = jnp.stack(others)
    order = jnp.stack([lax.rem(row - m + ratio, ratio) for m in range(ratio)])
    other = stacked[order].reshape(ratio, first_count, first_count, virtual, virtual)
    other = other.transpose(2, 0, 1, 4, 3)
    other = other.reshape(first_count, second_count, virtual, virtual)
    total = raw.reshape(first_count, second_count, virtual, virtual) + other
    return close(total, amplitudes, fock_vir, eps_occ, eps_vir)


def close(total, amplitudes, fock_vir, eps_occ, eps_vir):
    high = lax.Precision.HIGH
    row = lax.axis_index("row")
    col = lax.axis_index("col")
    first_count, second_count = amplitudes.shape[:2]
    total = total + jnp.einsum("ijac,cb->ijab", amplitudes, fock_vir, precision=high)
    total = total + jnp.einsum("ac,ijcb->ijab", fock_vir, amplitudes, precision=high)
    energy_rows = lax.dynamic_slice_in_dim(eps_occ, row * first_count, first_count)
    energy_cols = lax.dynamic_slice_in_dim(eps_occ, col * second_count, second_count)
    denominator = (
        energy_rows[:, None, None, None]
        + energy_cols[None, :, None, None]
        - eps_vir[None, None, :, None]
        - eps_vir[None, None, None, :]
    )
    return total / denominator


def plain(amplitudes, vvvv, hole_ints, exchange_ints, fock_occ, fock_vir, eps_occ, eps_vir):
    high = lax.Precision.HIGH
    rows_n = lax.axis_size("row")
    cols_n = lax.axis_size("col")
    row = lax.axis_index("row")
    col = lax.axis_index("col")
    first_count, second_count, virtual = amplitudes.shape[:3]
    occupied = fock_occ.shape[0]
    pairs_n = occupied * occupied
    a_count = vvvv.shape[0]
    c_count = vvvv.shape[2]
    k_count = exchange_ints.shape[0]

    split = lax.all_to_all(amplitudes, "col", split_axis=2, concat_axis=1, tiled=True)
    split = split.reshape(first_count * occupied, c_count * virtual)
    gathered = lax.all_gather(split, "row", axis=0, tiled=True)
    gathered = gathered.reshape(occupied, occupied, c_count, virtual)

    chi_part = lax.dot_general(
        gathered, exchange_ints, (((2, 3), (2, 3)), ((), ())), precision=high
    )
    chi_part = chi_part.reshape(pairs_n, k_count * occupied).T
    chi_all = lax.all_gather(chi_part, ("row", "col"), axis=0)
    chi = chi_all.reshape(rows_n, cols_n, k_count * occupied, pairs_n).sum(axis=1)
    delta = jnp.eye(occupied, dtype=fock_occ.dtype)
    known = hole_ints - delta[:, None, :, None] * fock_occ[None, :, None, :]
    mixing = chi.reshape(pairs_n, pairs_n) + known.reshape(pairs_n, pairs_n)

    mine = lax.dynamic_slice_in_dim(gathered, row * a_count, a_count, axis=3)
    mine = mine.transpose(1, 0, 3, 2).reshape(pairs_n, a_count * c_count)
    placed = lax.all_gather(mine, "col", axis=0)
    placed = placed.reshape(cols_n, pairs_n, a_count, c_count).transpose(1, 2, 0, 3)
    placed = placed.reshape(pairs_n, a_count * virtual)

    part = lax.dot_general(gathered, vvvv, (((2, 3), (2, 3)), ((), ())), precision=high)
    part = part.transpose(1, 0, 2, 3).reshape(occupied, occupied, a_count * virtual)
    raw = lax.psum_scatter(part, "col", scatter_dimension=0, tiled=True)
    chosen = lax.dynamic_slice_in_dim(
        mixing.reshape(pairs_n, occupied, occupied), col * second_count, second_count, axis=2
    )
    chosen = chosen.transpose(0, 2, 1).reshape(pairs_n, second_count * occupied)
    hole = lax.dot_general(chosen, placed, (((0,), (0,)), ((), ())), precision=high)
    raw = raw + hole.reshape(raw.shape)
    raw = raw.reshape(second_count, rows_n, first_count, a_count * virtual)
    raw = raw.transpose(1, 2, 0, 3)
    raw = lax.all_to_all(raw, "row", split_axis=0, concat_axis=0, tiled=True)
    raw = raw.transpose(1, 2, 0, 3).reshape(first_count, second_count, virtual * virtual)

    return finish(raw, amplitudes, fock_vir, eps_occ, eps_vir)


F32 = jnp.float32
BF16 = jnp.bfloat16


def split(x):
    high = x.astype(BF16)
    return high, (x - high.astype(F32)).astype(BF16)


def product(a, b, dims):
    return lax.dot_general(a, b, (dims, ((), ())), preferred_element_type=F32)


MESH = pl.DeviceIdType.MESH


def remote(source, target, send, recv, r, q):
    return pltpu.make_async_remote_copy(
        src_ref=source, dst_ref=target, send_sem=send, recv_sem=recv, device_id=(r, q), device_id_type=MESH
    )


def greet(row, col, rows_n, cols_n):
    barrier = pltpu.get_barrier_semaphore()
    for k in range(1, cols_n):
        pl.semaphore_signal(barrier, inc=1, device_id=(row, (col + k) % cols_n), device_id_type=MESH)
    for k in range(1, rows_n):
        pl.semaphore_signal(barrier, inc=1, device_id=((row + k) % rows_n, col), device_id_type=MESH)
    pl.semaphore_wait(barrier, cols_n - 1 + rows_n - 1)


def ladder_kernel(
    take, slots, x_ref, v_ref, e_ref, t_ref, o_ref, chi_ref,
    buf, rest, e_main, e_rest, e_spread, e_high, e_low, chi_sum, chi_got, spread, high, low, w_high, w_low,
    sem, own, send_a, recv_a, send_u, recv_u, send_d, recv_d, send_c, recv_c, send_p, recv_p, send_r, recv_r,
):
    a_count, b_count, c_count, virtual = v_ref.shape
    rows_n, chunks, cols_n, n, width = t_ref.shape
    levels = rows_n // 2
    row, col = lax.axis_index("row"), lax.axis_index("col")
    level, core = row // 2, row % 2
    twin = row + 1 - 2 * core
    group, lanes = buf.shape[3], buf.shape[4]
    tail = virtual - lanes
    rows = take * b_count
    blocks = a_count // take
    steps = chunks * blocks
    per = lanes // tail
    few = e_ref.shape[0] * e_ref.shape[1]
    dims = ((1,), (1,))

    def fetch(step):
        slot = lax.rem(step, slots)
        chunk, block = step // blocks, lax.rem(step, blocks)
        source = v_ref.at[
            pl.ds(block * take, take), :, pl.ds(pl.multiple_of(chunk * group, group), group), :
        ]
        return (
            pltpu.make_async_copy(source.at[:, :, :, pl.ds(0, lanes)], buf.at[slot], sem.at[slot, 0]),
            pltpu.make_async_copy(source.at[:, :, :, pl.ds(lanes, tail)], rest.at[slot], sem.at[slot, 1]),
        )

    def fetch_few():
        return (
            pltpu.make_async_copy(e_ref.at[:, :, :, pl.ds(0, lanes)], e_main, own.at[chunks]),
            pltpu.make_async_copy(e_ref.at[:, :, :, pl.ds(lanes, tail)], e_rest, own.at[chunks + 1]),
        )

    def keep(c):
        return pltpu.make_async_copy(x_ref.at[col, c], t_ref.at[row, c, col], own.at[c])

    def deal(k, c):
        q = (col + k) % cols_n
        return remote(x_ref.at[q, c], t_ref.at[row, c, col], send_a.at[c, k], recv_a.at[c, k], row, q)

    def dealt(k, c):
        q = (col + cols_n - k) % cols_n
        return remote(x_ref.at[col, c], t_ref.at[row, c, q], send_a.at[c, k], recv_a.at[c, k], row, q)

    def up(k, c):
        at = t_ref.at[jnp.maximum(row - 2 * k, core), c]
        return remote(at, at, send_u.at[c, k], recv_u.at[c, k], jnp.minimum(row + 2, rows_n - 2 + core), col)

    def down(k, c):
        at = t_ref.at[jnp.minimum(row + 2 * k, rows_n - 2 + core), c]
        return remote(at, at, send_d.at[c, k], recv_d.at[c, k], jnp.maximum(row - 2, core), col)

    def came_up(k, c):
        at = t_ref.at[jnp.maximum(row - 2 * k, core), c]
        return remote(at, at, send_u.at[c, k - 1], recv_u.at[c, k - 1], jnp.maximum(row - 2, core), col)

    def came_down(k, c):
        at = t_ref.at[jnp.minimum(row + 2 * k, rows_n - 2 + core), c]
        return remote(at, at, send_d.at[c, k - 1], recv_d.at[c, k - 1], jnp.minimum(row + 2, rows_n - 2 + core), col)

    def share(m, c):
        at = t_ref.at[2 * m + core, c]
        return remote(at, at, send_c.at[c, m], recv_c.at[c, m], twin, col)

    def shared(m, c):
        at = t_ref.at[2 * m + 1 - core, c]
        return remote(at, at, send_c.at[c, m], recv_c.at[c, m], twin, col)

    def open_up(c):
        keep(c).wait()
        for k in range(1, cols_n):
            dealt(k, c).wait_recv()

        @pl.when(level < levels - 1)
        def _():
            up(0, c).start()

        @pl.when(level > 0)
        def _():
            down(0, c).start()

        share(level, c).start()

    def relay(k, c):
        @pl.when(level >= k)
        def _():
            came_up(k, c).wait_recv()

            @pl.when(level < levels - 1)
            def _():
                up(k, c).start()

            share(level - k, c).start()

        @pl.when(level + k <= levels - 1)
        def _():
            came_down(k, c).wait_recv()

            @pl.when(level > 0)
            def _():
                down(k, c).start()

            share(level + k, c).start()

    def settle(c):
        for m in range(levels):
            shared(m, c).wait_recv()

    def plane(k):
        q = (col + k) % cols_n
        return remote(chi_sum, chi_got.at[k], send_p.at[k], recv_p.at[k], row, q)

    def column(k):
        r = (row + k) % rows_n
        return remote(chi_ref.at[row], chi_ref.at[row], send_r.at[k], recv_r.at[k], r, col)

    def columned(k):
        r = (row + rows_n - k) % rows_n
        return remote(chi_ref.at[r], chi_ref.at[r], send_r.at[k], recv_r.at[k], r, col)

    for step in range(slots - 1):
        for copy in fetch(step):
            copy.start()
    for copy in fetch_few():
        copy.start()
    greet(row, col, rows_n, cols_n)
    for c in range(chunks):
        keep(c).start()
        for k in range(1, cols_n):
            deal(k, c).start()
    o_ref[...] = jnp.zeros_like(o_ref)
    chi_sum[...] = jnp.zeros_like(chi_sum)
    for copy in fetch_few():
        copy.wait()
    open_up(0)
    open_up(1)
    for k in range(1, levels):
        relay(k, 0)
    settle(0)

    def lay(main, spread, start, stride, count, high, low):
        lane = lax.broadcasted_iota(jnp.int32, (count, lanes), 1)
        packed = None
        for c in range(group):
            hi, lo = split(main[pl.ds(start + c, count, stride=stride), :])
            high[:, c * lanes : (c + 1) * lanes] = hi
            low[:, c * lanes : (c + 1) * lanes] = lo
            piece = spread[pl.ds(start + c, count, stride=stride), :]
            k = c % per
            packed = piece if k == 0 else jnp.where(lane < tail * k, packed, pltpu.roll(piece, tail * k, 1))
            if k == per - 1:
                at = (group + c // per) * lanes
                hi, lo = split(packed)
                high[:, at : at + lanes] = hi
                low[:, at : at + lanes] = lo

    def triple(high, low):
        return (
            product(high[...], w_high[...], dims)
            + product(low[...], w_high[...], dims)
            + product(high[...], w_low[...], dims)
        )

    e_spread[:, pl.ds(0, tail)] = e_rest.reshape(few * c_count, tail)[...]

    def body(step, _):
        slot = lax.rem(step, slots)
        chunk, block = step // blocks, lax.rem(step, blocks)
        for copy in fetch(step):
            copy.wait()

        @pl.when(step + slots - 1 < steps)
        def _():
            for copy in fetch(step + slots - 1):
                copy.start()

        @pl.when(block == 0)
        def _():
            @pl.when(chunk + 1 < chunks)
            def _():
                relay(1, chunk + 1)

            @pl.when(chunk + 2 < chunks)
            def _():
                open_up(chunk + 2)

            for r in range(rows_n):
                for q in range(cols_n):
                    at = (r * cols_n + q) * n
                    hi, lo = split(t_ref[r, chunk, q])
                    w_high[at : at + n, :] = hi
                    w_low[at : at + n, :] = lo
            lay(
                e_main.reshape(few * c_count, lanes), e_spread, chunk * group, c_count, few, e_high, e_low
            )
            chi_sum[...] += triple(e_high, e_low)

            @pl.when(chunk == chunks - 1)
            def _():
                for k in range(1, cols_n):
                    plane(k).start()

        @pl.when(chunk + 1 < chunks)
        def _():
            for k in range(2, levels):
                @pl.when(block == min(2 * (k - 1), blocks - 1))
                def _():
                    relay(k, chunk + 1)

        @pl.when((chunk == chunks - 1) & (block == 2))
        def _():
            total = chi_sum[...]
            for k in range(1, cols_n):
                plane(k).wait_recv()
                total = total + chi_got[k]
            chi_ref[row] = total
            for k in range(1, rows_n):
                column(k).start()

        spread[:, pl.ds(0, tail)] = rest.at[slot].reshape(rows * group, tail)[...]
        lay(buf.at[slot].reshape(rows * group, lanes), spread, 0, group, rows, high, low)
        o_ref[pl.ds(pl.multiple_of(block * rows, rows), rows), :] += triple(high, low)

        @pl.when((block == blocks - 1) & (chunk + 1 < chunks))
        def _():
            settle(chunk + 1)

        return 0

    lax.fori_loop(0, steps, body, 0)
    for k in range(1, cols_n):
        plane(k).wait_send()
    for k in range(1, rows_n):
        column(k).wait_send()
        columned(k).wait_recv()
    for c in range(chunks):
        for k in range(1, cols_n):
            deal(k, c).wait_send()
        for m in range(levels):
            share(m, c).wait_send()
        for k in range(levels - 1):
            @pl.when((level >= k) & (level < levels - 1))
            def _():
                up(k, c).wait_send()

            @pl.when((level + k <= levels - 1) & (level > 0))
            def _():
                down(k, c).wait_send()


def ladder(x, v, e, rows_n, take, slots):
    a_count, b_count, c_count, virtual = v.shape
    cols_n, chunks, n, width = x.shape
    pairs = rows_n * cols_n * n
    group, lanes = c_count // chunks, 128
    tail = virtual - lanes
    rows = take * b_count
    few = e.shape[0] * e.shape[1]
    levels = rows_n // 2
    dma = pltpu.SemaphoreType.DMA
    vmem = pl.BlockSpec(memory_space=pltpu.VMEM)
    hbm = pl.BlockSpec(memory_space=pl.ANY)
    return pl.pallas_call(
        functools.partial(ladder_kernel, take, slots),
        out_shape=[
            jax.ShapeDtypeStruct((rows_n, chunks, cols_n, n, width), F32),
            jax.ShapeDtypeStruct((a_count * b_count, pairs), F32),
            jax.ShapeDtypeStruct((rows_n, few, pairs), F32),
        ],
        in_specs=[vmem, hbm, hbm],
        out_specs=[vmem] * 3,
        scratch_shapes=[
            pltpu.VMEM((slots, take, b_count, group, lanes), F32),
            pltpu.VMEM((slots, take, b_count, group, tail), F32),
            pltpu.VMEM(e.shape[:3] + (lanes,), F32),
            pltpu.VMEM(e.shape[:3] + (tail,), F32),
            pltpu.VMEM((few * c_count, lanes), F32),
            pltpu.VMEM((few, width), BF16),
            pltpu.VMEM((few, width), BF16),
            pltpu.VMEM((few, pairs), F32),
            pltpu.VMEM((cols_n, few, pairs), F32),
            pltpu.VMEM((rows * group, lanes), F32),
            pltpu.VMEM((rows, width), BF16),
            pltpu.VMEM((rows, width), BF16),
            pltpu.VMEM((pairs, width), BF16),
            pltpu.VMEM((pairs, width), BF16),
            dma((slots, 2)), dma((chunks + 2,)),
            dma((chunks, cols_n)), dma((chunks, cols_n)),
            dma((chunks, levels)), dma((chunks, levels)),
            dma((chunks, levels)), dma((chunks, levels)),
            dma((chunks, levels)), dma((chunks, levels)),
            dma((cols_n,)), dma((cols_n,)),
            dma((rows_n,)), dma((rows_n,)),
        ],
        compiler_params=pltpu.CompilerParams(
            collective_id=0, has_side_effects=True, vmem_limit_bytes=60 << 20
        ),
    )(x, v, e)


def hole_kernel(a_count, c_count, virtual, part_ref, t_ref, mixing_ref, o_ref, w_high, w_low, picked, add):
    rows_n, chunks, cols_n, n, width = t_ref.shape
    pairs = rows_n * cols_n * n
    lanes = 128
    tail = virtual - lanes
    group = c_count // chunks
    per = lanes // tail
    b_count = part_ref.shape[0] // a_count
    row, col = lax.axis_index("row"), lax.axis_index("col")
    up = -(-a_count // 16) * 16
    spot = row * a_count + lax.broadcasted_iota(jnp.int32, (up, lanes), 0)
    lane = lax.broadcasted_iota(jnp.int32, (up, lanes), 1)
    first = jnp.where(spot == lane, 1.0, 0.0).astype(BF16)
    later = [jnp.where(spot - lanes == lane - k * tail, 1.0, 0.0) for k in range(per)]
    later = [
        jnp.where((lane >= k * tail) & (lane < (k + 1) * tail), later[k], 0.0).astype(BF16)
        for k in range(per)
    ]
    dims = ((1,), (1,))
    for chunk in range(chunks):
        for r in range(rows_n):
            for q in range(cols_n):
                at = (r * cols_n + q) * n
                hi, lo = split(t_ref[r, chunk, q])
                w_high[at : at + n, :] = hi
                w_low[at : at + n, :] = lo
        for c in range(group):
            at = (group + c // per) * lanes
            k = c % per
            total = None
            for w in (w_high, w_low):
                value = product(first, w[:, c * lanes : (c + 1) * lanes], dims)
                value += product(later[k], w[:, at : at + lanes], dims)
                total = value if total is None else total + value
            for half in range(pairs // lanes):
                picked[half, pl.ds(chunk * group + c, a_count, stride=c_count), :] = total[
                    :a_count, half * lanes : (half + 1) * lanes
                ]
    mix_high, mix_low = split(mixing_ref[...])
    total = None
    for half in range(pairs // lanes):
        hi, lo = split(picked[half])
        at = slice(half * lanes, (half + 1) * lanes)
        value = (
            product(hi, mix_high[at, :], ((1,), (0,)))
            + product(lo, mix_high[at, :], ((1,), (0,)))
            + product(hi, mix_low[at, :], ((1,), (0,)))
        )
        total = value if total is None else total + value
    add[...] = part_ref[...]
    for a in range(a_count):
        at = pl.ds(pl.multiple_of(a * b_count + col * c_count, 8), c_count)
        add[at, :] += total[a * c_count : (a + 1) * c_count, :]
    step = 5 * lanes
    for block in range(part_ref.shape[0] // step):
        turned = add[block * step : (block + 1) * step, :].T
        for r in range(rows_n):
            for q in range(cols_n):
                at = (r * cols_n + q) * n
                for h in range(2):
                    o_ref[q, r, h, :, block * step : (block + 1) * step] = turned[
                        at + h * n // 2 : at + (h + 1) * n // 2, :
                    ]


def hole(part, t, mixing, a_count, c_count, virtual):
    rows_n, chunks, cols_n, n, width = t.shape
    pairs = rows_n * cols_n * n
    return pl.pallas_call(
        functools.partial(hole_kernel, a_count, c_count, virtual),
        out_shape=jax.ShapeDtypeStruct((cols_n, rows_n, 2, n // 2, part.shape[0]), F32),
        in_specs=[pl.BlockSpec(memory_space=pltpu.VMEM)] * 3,
        out_specs=pl.BlockSpec(memory_space=pltpu.VMEM),
        scratch_shapes=[
            pltpu.VMEM((pairs, width), BF16),
            pltpu.VMEM((pairs, width), BF16),
            pltpu.VMEM((pairs // 128, a_count * c_count, 128), F32),
            pltpu.VMEM(part.shape, F32),
        ],
        compiler_params=pltpu.CompilerParams(vmem_limit_bytes=60 << 20),
    )(part, t, mixing)


def exchange_kernel(
    part_ref, straight_ref, turned_ref, got, last, onward, sums, middle,
    send_a, recv_a, send_b, recv_b, send_c, recv_c, send_d, recv_d, send_e, recv_e, own,
):
    cols_n, rows_n = part_ref.shape[:2]
    row, col = lax.axis_index("row"), lax.axis_index("col")
    flips = (col + 1 - 2 * (col % 2), (col + 2) % 4)
    far = 3 - col

    def remote(source, target, send, recv, r, q):
        return pltpu.make_async_remote_copy(
            src_ref=source, dst_ref=target, send_sem=send, recv_sem=recv,
            device_id=(r, q), device_id_type=pl.DeviceIdType.MESH,
        )

    barrier = pltpu.get_barrier_semaphore()
    for q in (flips[0], flips[1], far):
        pl.semaphore_signal(barrier, inc=1, device_id=(row, q), device_id_type=pl.DeviceIdType.MESH)
    for k in range(1, rows_n):
        r = (row + k) % rows_n
        pl.semaphore_signal(barrier, inc=1, device_id=(r, col), device_id_type=pl.DeviceIdType.MESH)
    pl.semaphore_wait(barrier, cols_n - 1 + rows_n - 1)

    def pair(k):
        return flips if k < rows_n // 2 else (flips[1], flips[0])

    def scatter(k):
        near = pair(k)[0]
        return [
            remote(part_ref.at[near, k], got.at[k, 0], send_a.at[k, 0], recv_a.at[k, 0], row, near),
            remote(part_ref.at[far, k], got.at[k, 1], send_a.at[k, 1], recv_a.at[k, 1], row, near),
        ]

    def pass_on(k):
        return remote(onward.at[k], last.at[k], send_b.at[k], recv_b.at[k], row, pair(k)[1])

    def deliver(k):
        return remote(sums.at[k], straight_ref.at[row], send_c.at[k], recv_c.at[row], k, col)

    def deliver_own(k):
        return pltpu.make_async_copy(sums.at[k], straight_ref.at[row], own.at[0])

    def cross(k):
        return remote(sums.at[k], middle.at[k % 2, col], send_d.at[k], recv_d.at[k % 2, col], row, k // 2)

    def cross_own(k):
        return pltpu.make_async_copy(sums.at[k], middle.at[k % 2, col], own.at[1 + k % 2])

    def spread(m, q, h):
        return remote(
            middle.at[m, q, h], turned_ref.at[row, m], send_e.at[m, q, h], recv_e.at[row, m], 2 * q + h, col
        )

    def spread_own(m, q, h):
        return pltpu.make_async_copy(middle.at[m, q, h], turned_ref.at[row, m], own.at[3 + m])

    order = [k for m in range(rows_n // 2) for k in (m, rows_n // 2 + m)]
    ahead = 4
    for k in order[:ahead]:
        for copy in scatter(k):
            copy.start()

    def first(k):
        for copy in scatter(k):
            copy.wait_recv()
        onward[k] = part_ref[pair(k)[1], k] + got[k, 1]
        sums[k] = part_ref[col, k] + got[k, 0]
        pass_on(k).start()

    def second(k):
        pass_on(k).wait_recv()
        sums[k] = sums[k] + last[k]

        @pl.when(row != k)
        def _():
            deliver(k).start()

        @pl.when(row == k)
        def _():
            deliver_own(k).start()

        @pl.when(col != k // 2)
        def _():
            cross(k).start()

        @pl.when(col == k // 2)
        def _():
            cross_own(k).start()

    for at, k in enumerate(order):
        if at + ahead < rows_n:
            for copy in scatter(order[at + ahead]):
                copy.start()
        first(k)
        if at >= 2:
            second(order[at - 2])
    for k in order[-2:]:
        second(k)

    def arrived(m, q):
        @pl.when(col != q)
        def _():
            remote(sums.at[0], middle.at[m, q], send_d.at[0], recv_d.at[m, q], row, q).wait_recv()

    for m in range(2):
        for k in range(cols_n):
            @pl.when(col == k)
            def _():
                cross_own(2 * k + m).wait()
    for m in range(2):
        for q in range(cols_n):
            arrived(m, q)
            for h in range(2):
                @pl.when(row != 2 * q + h)
                def _():
                    spread(m, q, h).start()

                @pl.when(row == 2 * q + h)
                def _():
                    spread_own(m, q, h).start()
    for k in range(rows_n):
        for copy in scatter(k):
            copy.wait_send()
        pass_on(k).wait_send()

        @pl.when(row != k)
        def _():
            deliver(k).wait_send()
            remote(sums.at[0], straight_ref.at[k], send_c.at[k], recv_c.at[k], k, col).wait_recv()
            for m in range(2):
                spread(m, k // 2, k % 2).wait_send()
                remote(
                    middle.at[m, 0, 0], turned_ref.at[k, m], send_e.at[m, 0, 0], recv_e.at[k, m], k, col
                ).wait_recv()

        @pl.when(row == k)
        def _():
            deliver_own(k).wait()
            for m in range(2):
                spread_own(m, k // 2, k % 2).wait()

        @pl.when(col != k // 2)
        def _():
            cross(k).wait_send()


def exchange(part):
    cols_n, rows_n, _, n, width = part.shape
    block = (2, n, width)
    dma = pltpu.SemaphoreType.DMA
    return pl.pallas_call(
        exchange_kernel,
        out_shape=[jax.ShapeDtypeStruct((rows_n,) + block, F32)] * 2,
        in_specs=[pl.BlockSpec(memory_space=pltpu.VMEM)],
        out_specs=[pl.BlockSpec(memory_space=pltpu.VMEM)] * 2,
        scratch_shapes=[
            pltpu.VMEM((rows_n, 2) + block, F32),
            pltpu.VMEM((rows_n,) + block, F32),
            pltpu.VMEM((rows_n,) + block, F32),
            pltpu.VMEM((rows_n,) + block, F32),
            pltpu.VMEM((2, cols_n) + block, F32),
            dma((rows_n, 2)), dma((rows_n, 2)),
            dma((rows_n,)), dma((rows_n,)),
            dma((rows_n,)), dma((rows_n,)),
            dma((rows_n,)), dma((2, cols_n)),
            dma((2, cols_n, 2)), dma((rows_n, 2)),
            dma((5,)),
        ],
        compiler_params=pltpu.CompilerParams(
            collective_id=1, has_side_effects=True, vmem_limit_bytes=40 << 20
        ),
    )(part)


def fast(amplitudes, vvvv, hole_ints, exchange_ints, fock_occ, fock_vir, eps_occ, eps_vir):
    high = lax.Precision.HIGH
    rows_n = lax.axis_size("row")
    cols_n = lax.axis_size("col")
    row = lax.axis_index("row")
    col = lax.axis_index("col")
    first, second, virtual = amplitudes.shape[:3]
    occupied = fock_occ.shape[0]
    pairs = occupied * occupied
    a_count, c_count = vvvv.shape[0], vvvv.shape[2]
    group, lanes = 8, 128
    tail = virtual - lanes
    chunks = c_count // group
    n = first * second

    half = second // 2
    x = amplitudes.reshape(first, 2, half, virtual, virtual).transpose(1, 0, 2, 3, 4)
    x = x.reshape(n, cols_n, chunks, group, virtual)
    x = jnp.concatenate(
        [
            x[..., :lanes].reshape(n, cols_n, chunks, group * lanes),
            x[..., lanes:].reshape(n, cols_n, chunks, group * tail),
        ],
        axis=-1,
    ).transpose(1, 2, 0, 3)
    t, part, chi = ladder(x, vvvv, exchange_ints, rows_n, 4, 3)
    chi = chi.reshape(pairs, pairs)
    delta = jnp.eye(occupied, dtype=fock_occ.dtype)
    known = hole_ints - delta[:, None, :, None] * fock_occ[None, :, None, :]
    highest = lax.Precision.HIGHEST
    one, two = jnp.divmod(jnp.arange(pairs, dtype=jnp.int32), occupied)

    def place(i, j):
        inner = (j % second) // half * (first * half) + (i % first) * half + j % half
        return ((i // first) * cols_n + j // second) * n + inner

    spots = jnp.arange(pairs, dtype=jnp.int32)
    turn = (place(one, two)[:, None] == spots[None, :]).astype(F32)
    move = (spots[:, None] == place(two, one)[None, :]).astype(F32)
    known = jnp.dot(known.reshape(pairs, pairs), turn, precision=highest)


    mixing = jnp.dot(move, chi + known, precision=highest)
    part = hole(part, t, mixing, a_count, c_count, virtual)
    straight, turned = exchange(part)
    straight = straight.reshape(rows_n, 2, first, half, a_count, virtual)
    straight = straight.transpose(2, 1, 3, 0, 4, 5).reshape(first, second, virtual, virtual)
    turned = turned.reshape(rows_n, 2, half, first, a_count, virtual)
    turned = turned.transpose(3, 1, 2, 5, 0, 4).reshape(first, second, virtual, virtual)
    return close(straight + turned, amplitudes, fock_vir, eps_occ, eps_vir)


def on_device(amplitudes, vvvv, *rest):
    virtual, b_count, c_count = amplitudes.shape[2], vvvv.shape[1], vvvv.shape[2]
    tail = virtual - 128
    fits = (
        virtual > 128
        and 128 % tail == 0
        and c_count % 8 == 0
        and (8 * tail) % 128 == 0
        and vvvv.shape[0] % 4 == 0
        and (4 * b_count) % 128 == 0
        and (amplitudes.shape[0] * amplitudes.shape[1]) % 8 == 0
        and amplitudes.shape[1] == 2 * amplitudes.shape[0]
        and lax.axis_size("row") == 2 * lax.axis_size("col")
        and lax.axis_size("col") == 4
    )
    return (fast if fits else plain)(amplitudes, vvvv, *rest)


def solution(mesh):
    in_specs = (
        P("row", "col", None, None),
        P("row", None, "col", None),
        P(),
        P("row", None, "col", None),
        P(),
        P(),
        P(),
        P(),
    )
    out_specs = P("row", "col", None, None)
    return jax.shard_map(
        on_device, mesh=mesh, in_specs=in_specs, out_specs=out_specs, check_vma=False
    )
```

```python
import functools

import jax
import jax.numpy as jnp
from jax import lax
from jax.experimental import pallas as pl
from jax.experimental.pallas import tpu as pltpu
from jax.sharding import PartitionSpec as P

def finish(raw, amplitudes, fock_vir, eps_occ, eps_vir):
    high = lax.Precision.HIGH
    rows_n = lax.axis_size("row")
    cols_n = lax.axis_size("col")
    row = lax.axis_index("row")
    col = lax.axis_index("col")
    first_count, second_count, virtual = amplitudes.shape[:3]
    ratio = second_count // first_count
    others = []
    for turn in range(ratio):
        route = []
        for r in range(rows_n):
            for q in range(cols_n):
                m = (r + turn) % ratio
                route.append((r * cols_n + q, (q * ratio + m) * cols_n + r // ratio))
        m = lax.rem(row + turn, ratio)
        block = lax.dynamic_slice_in_dim(raw, m * first_count, first_count, axis=1)
        others.append(lax.ppermute(block, ("row", "col"), route))
    stacked = jnp.stack(others)
    order = jnp.stack([lax.rem(row - m + ratio, ratio) for m in range(ratio)])
    other = stacked[order].reshape(ratio, first_count, first_count, virtual, virtual)
    other = other.transpose(2, 0, 1, 4, 3)
    other = other.reshape(first_count, second_count, virtual, virtual)
    total = raw.reshape(first_count, second_count, virtual, virtual) + other
    return close(total, amplitudes, fock_vir, eps_occ, eps_vir)


def close(total, amplitudes, fock_vir, eps_occ, eps_vir):
    high = lax.Precision.HIGH
    row = lax.axis_index("row")
    col = lax.axis_index("col")
    first_count, second_count = amplitudes.shape[:2]
    total = total + jnp.einsum("ijac,cb->ijab", amplitudes, fock_vir, precision=high)
    total = total + jnp.einsum("ac,ijcb->ijab", fock_vir, amplitudes, precision=high)
    energy_rows = lax.dynamic_slice_in_dim(eps_occ, row * first_count, first_count)
    energy_cols = lax.dynamic_slice_in_dim(eps_occ, col * second_count, second_count)
    denominator = (
        energy_rows[:, None, None, None]
        + energy_cols[None, :, None, None]
        - eps_vir[None, None, :, None]
        - eps_vir[None, None, None, :]
    )
    return total / denominator


def plain(amplitudes, vvvv, hole_ints, exchange_ints, fock_occ, fock_vir, eps_occ, eps_vir):
    high = lax.Precision.HIGH
    rows_n = lax.axis_size("row")
    cols_n = lax.axis_size("col")
    row = lax.axis_index("row")
    col = lax.axis_index("col")
    first_count, second_count, virtual = amplitudes.shape[:3]
    occupied = fock_occ.shape[0]
    pairs_n = occupied * occupied
    a_count = vvvv.shape[0]
    c_count = vvvv.shape[2]
    k_count = exchange_ints.shape[0]

    split = lax.all_to_all(amplitudes, "col", split_axis=2, concat_axis=1, tiled=True)
    split = split.reshape(first_count * occupied, c_count * virtual)
    gathered = lax.all_gather(split, "row", axis=0, tiled=True)
    gathered = gathered.reshape(occupied, occupied, c_count, virtual)

    chi_part = lax.dot_general(
        gathered, exchange_ints, (((2, 3), (2, 3)), ((), ())), precision=high
    )
    chi_part = chi_part.reshape(pairs_n, k_count * occupied).T
    chi_all = lax.all_gather(chi_part, ("row", "col"), axis=0)
    chi = chi_all.reshape(rows_n, cols_n, k_count * occupied, pairs_n).sum(axis=1)
    delta = jnp.eye(occupied, dtype=fock_occ.dtype)
    known = hole_ints - delta[:, None, :, None] * fock_occ[None, :, None, :]
    mixing = chi.reshape(pairs_n, pairs_n) + known.reshape(pairs_n, pairs_n)

    mine = lax.dynamic_slice_in_dim(gathered, row * a_count, a_count, axis=3)
    mine = mine.transpose(1, 0, 3, 2).reshape(pairs_n, a_count * c_count)
    placed = lax.all_gather(mine, "col", axis=0)
    placed = placed.reshape(cols_n, pairs_n, a_count, c_count).transpose(1, 2, 0, 3)
    placed = placed.reshape(pairs_n, a_count * virtual)

    part = lax.dot_general(gathered, vvvv, (((2, 3), (2, 3)), ((), ())), precision=high)
    part = part.transpose(1, 0, 2, 3).reshape(occupied, occupied, a_count * virtual)
    raw = lax.psum_scatter(part, "col", scatter_dimension=0, tiled=True)
    chosen = lax.dynamic_slice_in_dim(
        mixing.reshape(pairs_n, occupied, occupied), col * second_count, second_count, axis=2
    )
    chosen = chosen.transpose(0, 2, 1).reshape(pairs_n, second_count * occupied)
    hole = lax.dot_general(chosen, placed, (((0,), (0,)), ((), ())), precision=high)
    raw = raw + hole.reshape(raw.shape)
    raw = raw.reshape(second_count, rows_n, first_count, a_count * virtual)
    raw = raw.transpose(1, 2, 0, 3)
    raw = lax.all_to_all(raw, "row", split_axis=0, concat_axis=0, tiled=True)
    raw = raw.transpose(1, 2, 0, 3).reshape(first_count, second_count, virtual * virtual)

    return finish(raw, amplitudes, fock_vir, eps_occ, eps_vir)


F32 = jnp.float32
BF16 = jnp.bfloat16


def split(x):
    high = x.astype(BF16)
    return high, (x - high.astype(F32)).astype(BF16)


def product(a, b, dims):
    return lax.dot_general(a, b, (dims, ((), ())), preferred_element_type=F32)


MESH = pl.DeviceIdType.MESH


def remote(source, target, send, recv, r, q):
    return pltpu.make_async_remote_copy(
        src_ref=source, dst_ref=target, send_sem=send, recv_sem=recv, device_id=(r, q), device_id_type=MESH
    )


def greet(row, col, rows_n, cols_n):
    barrier = pltpu.get_barrier_semaphore()
    for k in range(1, cols_n):
        pl.semaphore_signal(barrier, inc=1, device_id=(row, (col + k) % cols_n), device_id_type=MESH)
    for k in range(1, rows_n):
        pl.semaphore_signal(barrier, inc=1, device_id=((row + k) % rows_n, col), device_id_type=MESH)
    pl.semaphore_wait(barrier, cols_n - 1 + rows_n - 1)


def whole_kernel(
    take, slots, late, x_ref, v_ref, e_ref, known_ref, move_ref, straight_ref, turned_ref,
    t_ref, o_ref, chi_ref, buf, rest, e_main, e_rest, e_spread, e_high, e_low, chi_sum, chi_got,
    spread, high, low, w_high, w_low, picked, part_ref, got, last, onward, sums, middle,
    sem, own, send_a, recv_a, send_u, recv_u, send_d, recv_d, send_c, recv_c, send_p, recv_p, send_r, recv_r,
    xsend_a, xrecv_a, xsend_b, xrecv_b, xsend_c, xrecv_c, xsend_d, xrecv_d, xsend_e, xrecv_e, xown,
):
    a_count, b_count, c_count, virtual = v_ref.shape
    rows_n, chunks, cols_n, n, width = t_ref.shape
    levels = rows_n // 2
    row, col = lax.axis_index("row"), lax.axis_index("col")
    level, core = row // 2, row % 2
    twin = row + 1 - 2 * core
    group, lanes = buf.shape[3], buf.shape[4]
    tail = virtual - lanes
    rows = take * b_count
    blocks = a_count // take
    steps = chunks * blocks
    per = lanes // tail
    few = e_ref.shape[0] * e_ref.shape[1]
    pairs = rows_n * cols_n * n
    early = chunks - late
    dims = ((1,), (1,))
    flips = (col + 1 - 2 * (col % 2), (col + 2) % 4)
    far = 3 - col

    def where(step):
        after = step - early * blocks
        is_late = step >= early * blocks
        chunk = jnp.where(is_late, early + lax.rem(jnp.maximum(after, 0), late), step // blocks)
        block = jnp.where(is_late, jnp.maximum(after, 0) // late, lax.rem(step, blocks))
        return chunk, block

    def fetch(step):
        slot = lax.rem(step, slots)
        chunk, block = where(step)
        source = v_ref.at[
            pl.ds(block * take, take), :, pl.ds(pl.multiple_of(chunk * group, group), group), :
        ]
        return (
            pltpu.make_async_copy(source.at[:, :, :, pl.ds(0, lanes)], buf.at[slot], sem.at[slot, 0]),
            pltpu.make_async_copy(source.at[:, :, :, pl.ds(lanes, tail)], rest.at[slot], sem.at[slot, 1]),
        )

    def fetch_few():
        return (
            pltpu.make_async_copy(e_ref.at[:, :, :, pl.ds(0, lanes)], e_main, own.at[chunks]),
            pltpu.make_async_copy(e_ref.at[:, :, :, pl.ds(lanes, tail)], e_rest, own.at[chunks + 1]),
        )

    def keep(c):
        return pltpu.make_async_copy(x_ref.at[col, c], t_ref.at[row, c, col], own.at[c])

    def deal(k, c):
        q = (col + k) % cols_n
        return remote(x_ref.at[q, c], t_ref.at[row, c, col], send_a.at[c, k], recv_a.at[c, k], row, q)

    def dealt(k, c):
        q = (col + cols_n - k) % cols_n
        return remote(x_ref.at[col, c], t_ref.at[row, c, q], send_a.at[c, k], recv_a.at[c, k], row, q)

    def up(k, c):
        at = t_ref.at[jnp.maximum(row - 2 * k, core), c]
        return remote(at, at, send_u.at[c, k], recv_u.at[c, k], jnp.minimum(row + 2, rows_n - 2 + core), col)

    def down(k, c):
        at = t_ref.at[jnp.minimum(row + 2 * k, rows_n - 2 + core), c]
        return remote(at, at, send_d.at[c, k], recv_d.at[c, k], jnp.maximum(row - 2, core), col)

    def came_up(k, c):
        at = t_ref.at[jnp.maximum(row - 2 * k, core), c]
        return remote(at, at, send_u.at[c, k - 1], recv_u.at[c, k - 1], jnp.maximum(row - 2, core), col)

    def came_down(k, c):
        at = t_ref.at[jnp.minimum(row + 2 * k, rows_n - 2 + core), c]
        return remote(at, at, send_d.at[c, k - 1], recv_d.at[c, k - 1], jnp.minimum(row + 2, rows_n - 2 + core), col)

    def share(m, c):
        at = t_ref.at[2 * m + core, c]
        return remote(at, at, send_c.at[c, m], recv_c.at[c, m], twin, col)

    def shared(m, c):
        at = t_ref.at[2 * m + 1 - core, c]
        return remote(at, at, send_c.at[c, m], recv_c.at[c, m], twin, col)

    def open_up(c):
        keep(c).wait()
        for k in range(1, cols_n):
            dealt(k, c).wait_recv()

        @pl.when(level < levels - 1)
        def _():
            up(0, c).start()

        @pl.when(level > 0)
        def _():
            down(0, c).start()

        share(level, c).start()

    def relay(k, c):
        @pl.when(level >= k)
        def _():
            came_up(k, c).wait_recv()

            @pl.when(level < levels - 1)
            def _():
                up(k, c).start()

            share(level - k, c).start()

        @pl.when(level + k <= levels - 1)
        def _():
            came_down(k, c).wait_recv()

            @pl.when(level > 0)
            def _():
                down(k, c).start()

            share(level + k, c).start()

    def settle(c):
        for m in range(levels):
            shared(m, c).wait_recv()

    def plane(k):
        q = (col + k) % cols_n
        return remote(chi_sum, chi_got.at[k], send_p.at[k], recv_p.at[k], row, q)

    def column(k):
        r = (row + k) % rows_n
        return remote(chi_ref.at[row], chi_ref.at[row], send_r.at[k], recv_r.at[k], r, col)

    def columned(k):
        r = (row + rows_n - k) % rows_n
        return remote(chi_ref.at[r], chi_ref.at[r], send_r.at[k], recv_r.at[k], r, col)

    for step in range(slots - 1):
        for copy in fetch(step):
            copy.start()
    for copy in fetch_few():
        copy.start()
    greet(row, col, rows_n, cols_n)
    for c in range(chunks):
        keep(c).start()
        for k in range(1, cols_n):
            deal(k, c).start()
    o_ref[...] = jnp.zeros_like(o_ref)
    chi_sum[...] = jnp.zeros_like(chi_sum)
    for copy in fetch_few():
        copy.wait()
    open_up(0)
    open_up(1)
    for k in range(1, levels):
        relay(k, 0)
    settle(0)

    def lay(main, spread, start, stride, count, high, low):
        lane = lax.broadcasted_iota(jnp.int32, (count, lanes), 1)
        packed = None
        for c in range(group):
            hi, lo = split(main[pl.ds(start + c, count, stride=stride), :])
            high[:, c * lanes : (c + 1) * lanes] = hi
            low[:, c * lanes : (c + 1) * lanes] = lo
            piece = spread[pl.ds(start + c, count, stride=stride), :]
            k = c % per
            packed = piece if k == 0 else jnp.where(lane < tail * k, packed, pltpu.roll(piece, tail * k, 1))
            if k == per - 1:
                at = (group + c // per) * lanes
                hi, lo = split(packed)
                high[:, at : at + lanes] = hi
                low[:, at : at + lanes] = lo

    def pair(k):
        return flips if k < rows_n // 2 else (flips[1], flips[0])

    def scatter(p, k):
        near = pair(k)[0]
        return [
            remote(part_ref.at[p, q, k], got.at[p, k, m], xsend_a.at[p, k, m], xrecv_a.at[p, k, m], row, near)
            for m, q in enumerate((near, far))
        ]

    def pass_on(p, k):
        return remote(onward.at[p, k], last.at[p, k], xsend_b.at[p, k], xrecv_b.at[p, k], row, pair(k)[1])

    def deliver(p, k):
        return remote(sums.at[p, k], straight_ref.at[row, p], xsend_c.at[p, k], xrecv_c.at[p, row], k, col)

    def delivered(p, k):
        return remote(sums.at[p, k], straight_ref.at[k, p], xsend_c.at[p, k], xrecv_c.at[p, k], k, col)

    def deliver_own(p, k):
        return pltpu.make_async_copy(sums.at[p, k], straight_ref.at[row, p], xown.at[p, 0])

    def cross(p, k):
        return remote(
            sums.at[p, k], middle.at[p, k % 2, col], xsend_d.at[p, k], xrecv_d.at[p, k % 2, col], row, k // 2
        )

    def crossed(p, m, q):
        return remote(sums.at[p, m], middle.at[p, m, q], xsend_d.at[p, m], xrecv_d.at[p, m, q], row, q)

    def cross_own(p, k):
        return pltpu.make_async_copy(sums.at[p, k], middle.at[p, k % 2, col], xown.at[p, 1 + k % 2])

    def fan(p, m, q, h):
        return remote(
            middle.at[p, m, q, h], turned_ref.at[row, p, m],
            xsend_e.at[p, m, q, h], xrecv_e.at[p, row, m], 2 * q + h, col,
        )

    def fanned(p, m, k):
        return remote(
            middle.at[p, m, k // 2, k % 2], turned_ref.at[k, p, m],
            xsend_e.at[p, m, k // 2, k % 2], xrecv_e.at[p, k, m], k, col,
        )

    def fan_own(p, m, q, h):
        return pltpu.make_async_copy(middle.at[p, m, q, h], turned_ref.at[row, p, m], xown.at[p, 3 + m])

    order = [k for m in range(rows_n // 2) for k in (m, rows_n // 2 + m)]

    def launch(p):
        turned = o_ref[pl.ds(pl.multiple_of(p * rows, rows), rows), :].T
        for r in range(rows_n):
            for q in range(cols_n):
                for h in range(2):
                    at = (r * cols_n + q) * n + h * n // 2
                    part_ref[p, q, r, h] = turned[at : at + n // 2, :]
        for k in order:
            for copy in scatter(p, k):
                copy.start()

    def first(p):
        for k in order:
            for copy in scatter(p, k):
                copy.wait_recv()
            onward[p, k] = part_ref[p, pair(k)[1], k] + got[p, k, 1]
            sums[p, k] = part_ref[p, col, k] + got[p, k, 0]
            pass_on(p, k).start()

    def second(p):
        for k in order:
            pass_on(p, k).wait_recv()
            sums[p, k] = sums[p, k] + last[p, k]

            @pl.when(col != k // 2)
            def _():
                cross(p, k).start()

            @pl.when(col == k // 2)
            def _():
                cross_own(p, k).start()

            @pl.when(row != k)
            def _():
                deliver(p, k).start()

            @pl.when(row == k)
            def _():
                deliver_own(p, k).start()

    def third(p):
        for k in order:
            m = k % 2

            @pl.when(col == k // 2)
            def _():
                cross_own(p, k).wait()
                for q in range(cols_n):
                    @pl.when(col != q)
                    def _():
                        crossed(p, m, q).wait_recv()

                    for h in range(2):
                        @pl.when(row != 2 * q + h)
                        def _():
                            fan(p, m, q, h).start()

                        @pl.when(row == 2 * q + h)
                        def _():
                            fan_own(p, m, q, h).start()

    def drain(p):
        for k in order:
            for copy in scatter(p, k):
                copy.wait_send()
            pass_on(p, k).wait_send()

            @pl.when(row != k)
            def _():
                deliver(p, k).wait_send()
                delivered(p, k).wait_recv()
                for m in range(2):
                    fan(p, m, k // 2, k % 2).wait_send()
                    fanned(p, m, k).wait_recv()

            @pl.when(row == k)
            def _():
                deliver_own(p, k).wait()
                for m in range(2):
                    fan_own(p, m, k // 2, k % 2).wait()

            @pl.when(col != k // 2)
            def _():
                cross(p, k).wait_send()

    def triple(high, low, w):
        return (
            product(high[...], w_high[w], dims)
            + product(low[...], w_high[w], dims)
            + product(high[...], w_low[w], dims)
        )

    e_spread[:, pl.ds(0, tail)] = e_rest.reshape(few * c_count, tail)[...]
    tall = -(-a_count // 16) * 16
    spot = row * a_count + lax.broadcasted_iota(jnp.int32, (tall, lanes), 0)
    lane = lax.broadcasted_iota(jnp.int32, (tall, lanes), 1)
    choose = jnp.where(spot == lane, 1.0, 0.0).astype(BF16)
    later = []
    for k in range(per):
        hit = (spot - lanes == lane - k * tail) & (lane >= k * tail) & (lane < (k + 1) * tail)
        later.append(jnp.where(hit, 1.0, 0.0).astype(BF16))

    def prepare(chunk, w):
        for r in range(rows_n):
            for q in range(cols_n):
                at = (r * cols_n + q) * n
                hi, lo = split(t_ref[r, chunk, q])
                w_high[w, at : at + n, :] = hi
                w_low[w, at : at + n, :] = lo
        for c in range(group):
            at = (group + c // per) * lanes
            total = None
            for ref in (w_high, w_low):
                value = product(choose, ref[w, :, c * lanes : (c + 1) * lanes], dims)
                value += product(later[c % per], ref[w, :, at : at + lanes], dims)
                total = value if total is None else total + value
            for half in range(pairs // lanes):
                picked[half, pl.ds(chunk * group + c, a_count, stride=c_count), :] = total[
                    :a_count, half * lanes : (half + 1) * lanes
                ]
        lay(e_main.reshape(few * c_count, lanes), e_spread, chunk * group, c_count, few, e_high, e_low)
        chi_sum[...] += triple(e_high, e_low, w)

    def multiply(step, block, w):
        slot = lax.rem(step, slots)
        for copy in fetch(step):
            copy.wait()

        @pl.when(step + slots - 1 < steps)
        def _():
            for copy in fetch(step + slots - 1):
                copy.start()

        spread[:, pl.ds(0, tail)] = rest.at[slot].reshape(rows * group, tail)[...]
        lay(buf.at[slot].reshape(rows * group, lanes), spread, 0, group, rows, high, low)
        o_ref[pl.ds(pl.multiple_of(block * rows, rows), rows), :] += triple(high, low, w)

    def opening(step, _):
        chunk, block = step // blocks, lax.rem(step, blocks)
        ahead = 1 + step // (levels - 1)

        @pl.when(ahead < chunks)
        def _():
            for k in range(1, levels):
                @pl.when(lax.rem(step, levels - 1) == k - 1)
                def _():
                    relay(k, ahead)

            @pl.when((lax.rem(step, levels - 1) == 0) & (ahead + 1 < chunks))
            def _():
                open_up(ahead + 1)

        @pl.when(block == 0)
        def _():
            prepare(chunk, 0)

        multiply(step, block, 0)

        @pl.when((block == blocks - 1) & (chunk + 1 < early))
        def _():
            settle(chunk + 1)

        return 0

    lax.fori_loop(0, early * blocks, opening, 0)
    for w in range(late):
        settle(early + w)
        prepare(early + w, w)
    for k in range(1, cols_n):
        plane(k).start()

    def hole():
        for k in range(1, rows_n):
            columned(k).wait_recv()
        turn_high = turn_low = None
        for r in range(rows_n):
            at = slice(r * few, (r + 1) * few)
            hi, lo = split(chi_ref[r] + known_ref[at, :])
            turn = move_ref[:, at]
            hi = product(turn, hi, ((1,), (0,)))
            lo = product(turn, lo, ((1,), (0,)))
            turn_high = hi if turn_high is None else turn_high + hi
            turn_low = lo if turn_low is None else turn_low + lo
        mix_high, mix_low = turn_high.astype(BF16), turn_low.astype(BF16)
        total = None
        for half in range(pairs // lanes):
            hi, lo = split(picked[half])
            at = slice(half * lanes, (half + 1) * lanes)
            value = (
                product(hi, mix_high[at, :], ((1,), (0,)))
                + product(lo, mix_high[at, :], ((1,), (0,)))
                + product(hi, mix_low[at, :], ((1,), (0,)))
            )
            total = value if total is None else total + value
        for a in range(a_count):
            at = pl.ds(pl.multiple_of(a * b_count + col * c_count, 8), c_count)
            o_ref[at, :] += total[a * c_count : (a + 1) * c_count, :]

    def closing(block, _):
        def inner(w, _):
            multiply(early * blocks + block * late + w, block, w)

            @pl.when((block == 0) & (w == 0))
            def _():
                total = chi_sum[...]
                for k in range(1, cols_n):
                    plane(k).wait_recv()
                    total = total + chi_got[k]
                chi_ref[row] = total
                for k in range(1, rows_n):
                    column(k).start()

            @pl.when((w == 0) & (block >= 1))
            def _():
                first(block - 1)

            return 0

        lax.fori_loop(0, late, inner, 0)

        @pl.when(block == 0)
        def _():
            hole()

        launch(block)

        @pl.when(block >= 1)
        def _():
            second(block - 1)

        @pl.when(block >= 2)
        def _():
            third(block - 2)

        return 0

    lax.fori_loop(0, blocks, closing, 0)
    third(blocks - 2)
    first(blocks - 1)
    second(blocks - 1)
    third(blocks - 1)
    lax.fori_loop(0, blocks, lambda p, _: (drain(p), 0)[1], 0)
    for k in range(1, cols_n):
        plane(k).wait_send()
    for k in range(1, rows_n):
        column(k).wait_send()
    for c in range(chunks):
        for k in range(1, cols_n):
            deal(k, c).wait_send()
        for m in range(levels):
            share(m, c).wait_send()
        for k in range(levels - 1):
            @pl.when((level >= k) & (level < levels - 1))
            def _():
                up(k, c).wait_send()

            @pl.when((level + k <= levels - 1) & (level > 0))
            def _():
                down(k, c).wait_send()


def whole(x, v, e, known, move, rows_n, take, slots, late):
    a_count, b_count, c_count, virtual = v.shape
    cols_n, chunks, n, width = x.shape
    pairs = rows_n * cols_n * n
    group, lanes = c_count // chunks, 128
    tail = virtual - lanes
    rows = take * b_count
    blocks = a_count // take
    few = e.shape[0] * e.shape[1]
    levels = rows_n // 2
    block = (2, n // 2, rows)
    dma = pltpu.SemaphoreType.DMA
    vmem = pl.BlockSpec(memory_space=pltpu.VMEM)
    hbm = pl.BlockSpec(memory_space=pl.ANY)
    return pl.pallas_call(
        functools.partial(whole_kernel, take, slots, late),
        out_shape=[jax.ShapeDtypeStruct((rows_n, blocks) + block, F32)] * 2,
        in_specs=[vmem, hbm, hbm, vmem, vmem],
        out_specs=[vmem] * 2,
        scratch_shapes=[
            pltpu.VMEM((rows_n, chunks, cols_n, n, width), F32),
            pltpu.VMEM((a_count * b_count, pairs), F32),
            pltpu.VMEM((rows_n, few, pairs), F32),
            pltpu.VMEM((slots, take, b_count, group, lanes), F32),
            pltpu.VMEM((slots, take, b_count, group, tail), F32),
            pltpu.VMEM(e.shape[:3] + (lanes,), F32),
            pltpu.VMEM(e.shape[:3] + (tail,), F32),
            pltpu.VMEM((few * c_count, lanes), F32),
            pltpu.VMEM((few, width), BF16),
            pltpu.VMEM((few, width), BF16),
            pltpu.VMEM((few, pairs), F32),
            pltpu.VMEM((cols_n, few, pairs), F32),
            pltpu.VMEM((rows * group, lanes), F32),
            pltpu.VMEM((rows, width), BF16),
            pltpu.VMEM((rows, width), BF16),
            pltpu.VMEM((late, pairs, width), BF16),
            pltpu.VMEM((late, pairs, width), BF16),
            pltpu.VMEM((pairs // lanes, a_count * c_count, lanes), F32),
            pltpu.VMEM((blocks, cols_n, rows_n) + block, F32),
            pltpu.VMEM((blocks, rows_n, 2) + block, F32),
            pltpu.VMEM((blocks, rows_n) + block, F32),
            pltpu.VMEM((blocks, rows_n) + block, F32),
            pltpu.VMEM((blocks, rows_n) + block, F32),
            pltpu.VMEM((blocks, 2, cols_n) + block, F32),
            dma((slots, 2)), dma((chunks + 2,)),
            dma((chunks, cols_n)), dma((chunks, cols_n)),
            dma((chunks, levels)), dma((chunks, levels)),
            dma((chunks, levels)), dma((chunks, levels)),
            dma((chunks, levels)), dma((chunks, levels)),
            dma((cols_n,)), dma((cols_n,)),
            dma((rows_n,)), dma((rows_n,)),
            dma((blocks, rows_n, 2)), dma((blocks, rows_n, 2)),
            dma((blocks, rows_n)), dma((blocks, rows_n)),
            dma((blocks, rows_n)), dma((blocks, rows_n)),
            dma((blocks, rows_n)), dma((blocks, 2, cols_n)),
            dma((blocks, 2, cols_n, 2)), dma((blocks, rows_n, 2)),
            dma((blocks, 5)),
        ],
        compiler_params=pltpu.CompilerParams(
            collective_id=0, has_side_effects=True, vmem_limit_bytes=62 << 20
        ),
    )(x, v, e, known, move)


def fast(amplitudes, vvvv, hole_ints, exchange_ints, fock_occ, fock_vir, eps_occ, eps_vir):
    high = lax.Precision.HIGH
    rows_n = lax.axis_size("row")
    cols_n = lax.axis_size("col")
    row = lax.axis_index("row")
    col = lax.axis_index("col")
    first, second, virtual = amplitudes.shape[:3]
    occupied = fock_occ.shape[0]
    pairs = occupied * occupied
    a_count, c_count = vvvv.shape[0], vvvv.shape[2]
    group, lanes = 8, 128
    tail = virtual - lanes
    chunks = c_count // group
    n = first * second

    half = second // 2
    x = amplitudes.reshape(first, 2, half, virtual, virtual).transpose(1, 0, 2, 3, 4)
    x = x.reshape(n, cols_n, chunks, group, virtual)
    x = jnp.concatenate(
        [
            x[..., :lanes].reshape(n, cols_n, chunks, group * lanes),
            x[..., lanes:].reshape(n, cols_n, chunks, group * tail),
        ],
        axis=-1,
    ).transpose(1, 2, 0, 3)
    delta = jnp.eye(occupied, dtype=fock_occ.dtype)
    known = hole_ints - delta[:, None, :, None] * fock_occ[None, :, None, :]
    highest = lax.Precision.HIGHEST
    one, two = jnp.divmod(jnp.arange(pairs, dtype=jnp.int32), occupied)

    def place(i, j):
        inner = (j % second) // half * (first * half) + (i % first) * half + j % half
        return ((i // first) * cols_n + j // second) * n + inner

    spots = jnp.arange(pairs, dtype=jnp.int32)
    turn = (place(one, two)[:, None] == spots[None, :]).astype(F32)
    move = (spots[:, None] == place(two, one)[None, :]).astype(F32)
    known = jnp.dot(known.reshape(pairs, pairs), turn, precision=highest)


    straight, turned = whole(x, vvvv, exchange_ints, known, move.astype(BF16), rows_n, 4, 3, 2)
    blocks = a_count // 4
    straight = straight.reshape(rows_n, blocks, 2, first, half, 4, virtual)
    straight = straight.transpose(3, 2, 4, 0, 1, 5, 6).reshape(first, second, virtual, virtual)
    turned = turned.reshape(rows_n, blocks, 2, half, first, 4, virtual)
    turned = turned.transpose(4, 2, 3, 6, 0, 1, 5).reshape(first, second, virtual, virtual)
    return close(straight + turned, amplitudes, fock_vir, eps_occ, eps_vir)


def on_device(amplitudes, vvvv, *rest):
    virtual, b_count, c_count = amplitudes.shape[2], vvvv.shape[1], vvvv.shape[2]
    tail = virtual - 128
    fits = (
        virtual > 128
        and 128 % tail == 0
        and c_count % 8 == 0
        and c_count >= 24
        and (c_count // 8 - 2) * (vvvv.shape[0] // 4) >= (c_count // 8 - 1) * (lax.axis_size("row") // 2 - 1)
        and (8 * tail) % 128 == 0
        and vvvv.shape[0] % 4 == 0
        and (4 * b_count) % 128 == 0
        and (amplitudes.shape[0] * amplitudes.shape[1]) % 8 == 0
        and amplitudes.shape[1] == 2 * amplitudes.shape[0]
        and lax.axis_size("row") == 2 * lax.axis_size("col")
        and lax.axis_size("col") == 4
    )
    return (fast if fits else plain)(amplitudes, vvvv, *rest)


def solution(mesh):
    in_specs = (
        P("row", "col", None, None),
        P("row", None, "col", None),
        P(),
        P("row", None, "col", None),
        P(),
        P(),
        P(),
        P(),
    )
    out_specs = P("row", "col", None, None)
    return jax.shard_map(
        on_device, mesh=mesh, in_specs=in_specs, out_specs=out_specs, check_vma=False
    )
```

```python
import functools

import jax
import jax.numpy as jnp
import numpy as np
from jax import lax
from jax.experimental import pallas as pl
from jax.experimental.pallas import tpu as pltpu
from jax.sharding import PartitionSpec as P

def finish(raw, amplitudes, fock_vir, eps_occ, eps_vir):
    high = lax.Precision.HIGH
    rows_n = lax.axis_size("row")
    cols_n = lax.axis_size("col")
    row = lax.axis_index("row")
    col = lax.axis_index("col")
    first_count, second_count, virtual = amplitudes.shape[:3]
    ratio = second_count // first_count
    others = []
    for turn in range(ratio):
        route = []
        for r in range(rows_n):
            for q in range(cols_n):
                m = (r + turn) % ratio
                route.append((r * cols_n + q, (q * ratio + m) * cols_n + r // ratio))
        m = lax.rem(row + turn, ratio)
        block = lax.dynamic_slice_in_dim(raw, m * first_count, first_count, axis=1)
        others.append(lax.ppermute(block, ("row", "col"), route))
    stacked = jnp.stack(others)
    order = jnp.stack([lax.rem(row - m + ratio, ratio) for m in range(ratio)])
    other = stacked[order].reshape(ratio, first_count, first_count, virtual, virtual)
    other = other.transpose(2, 0, 1, 4, 3)
    other = other.reshape(first_count, second_count, virtual, virtual)
    total = raw.reshape(first_count, second_count, virtual, virtual) + other
    return close(total, amplitudes, fock_vir, eps_occ, eps_vir)


def close(total, amplitudes, fock_vir, eps_occ, eps_vir):
    high = lax.Precision.HIGH
    row = lax.axis_index("row")
    col = lax.axis_index("col")
    first_count, second_count = amplitudes.shape[:2]
    total = total + jnp.einsum("ijac,cb->ijab", amplitudes, fock_vir, precision=high)
    total = total + jnp.einsum("ac,ijcb->ijab", fock_vir, amplitudes, precision=high)
    energy_rows = lax.dynamic_slice_in_dim(eps_occ, row * first_count, first_count)
    energy_cols = lax.dynamic_slice_in_dim(eps_occ, col * second_count, second_count)
    denominator = (
        energy_rows[:, None, None, None]
        + energy_cols[None, :, None, None]
        - eps_vir[None, None, :, None]
        - eps_vir[None, None, None, :]
    )
    return total / denominator


def plain(amplitudes, vvvv, hole_ints, exchange_ints, fock_occ, fock_vir, eps_occ, eps_vir):
    high = lax.Precision.HIGH
    rows_n = lax.axis_size("row")
    cols_n = lax.axis_size("col")
    row = lax.axis_index("row")
    col = lax.axis_index("col")
    first_count, second_count, virtual = amplitudes.shape[:3]
    occupied = fock_occ.shape[0]
    pairs_n = occupied * occupied
    a_count = vvvv.shape[0]
    c_count = vvvv.shape[2]
    k_count = exchange_ints.shape[0]

    split = lax.all_to_all(amplitudes, "col", split_axis=2, concat_axis=1, tiled=True)
    split = split.reshape(first_count * occupied, c_count * virtual)
    gathered = lax.all_gather(split, "row", axis=0, tiled=True)
    gathered = gathered.reshape(occupied, occupied, c_count, virtual)

    chi_part = lax.dot_general(
        gathered, exchange_ints, (((2, 3), (2, 3)), ((), ())), precision=high
    )
    chi_part = chi_part.reshape(pairs_n, k_count * occupied).T
    chi_all = lax.all_gather(chi_part, ("row", "col"), axis=0)
    chi = chi_all.reshape(rows_n, cols_n, k_count * occupied, pairs_n).sum(axis=1)
    delta = jnp.eye(occupied, dtype=fock_occ.dtype)
    known = hole_ints - delta[:, None, :, None] * fock_occ[None, :, None, :]
    mixing = chi.reshape(pairs_n, pairs_n) + known.reshape(pairs_n, pairs_n)

    mine = lax.dynamic_slice_in_dim(gathered, row * a_count, a_count, axis=3)
    mine = mine.transpose(1, 0, 3, 2).reshape(pairs_n, a_count * c_count)
    placed = lax.all_gather(mine, "col", axis=0)
    placed = placed.reshape(cols_n, pairs_n, a_count, c_count).transpose(1, 2, 0, 3)
    placed = placed.reshape(pairs_n, a_count * virtual)

    part = lax.dot_general(gathered, vvvv, (((2, 3), (2, 3)), ((), ())), precision=high)
    part = part.transpose(1, 0, 2, 3).reshape(occupied, occupied, a_count * virtual)
    raw = lax.psum_scatter(part, "col", scatter_dimension=0, tiled=True)
    chosen = lax.dynamic_slice_in_dim(
        mixing.reshape(pairs_n, occupied, occupied), col * second_count, second_count, axis=2
    )
    chosen = chosen.transpose(0, 2, 1).reshape(pairs_n, second_count * occupied)
    hole = lax.dot_general(chosen, placed, (((0,), (0,)), ((), ())), precision=high)
    raw = raw + hole.reshape(raw.shape)
    raw = raw.reshape(second_count, rows_n, first_count, a_count * virtual)
    raw = raw.transpose(1, 2, 0, 3)
    raw = lax.all_to_all(raw, "row", split_axis=0, concat_axis=0, tiled=True)
    raw = raw.transpose(1, 2, 0, 3).reshape(first_count, second_count, virtual * virtual)

    return finish(raw, amplitudes, fock_vir, eps_occ, eps_vir)


F32 = jnp.float32
BF16 = jnp.bfloat16


def split(x):
    high = x.astype(BF16)
    return high, (x - high.astype(F32)).astype(BF16)


def product(a, b, dims):
    return lax.dot_general(a, b, (dims, ((), ())), preferred_element_type=F32)


MESH = pl.DeviceIdType.MESH


def remote(source, target, send, recv, r, q):
    return pltpu.make_async_remote_copy(
        src_ref=source, dst_ref=target, send_sem=send, recv_sem=recv, device_id=(r, q), device_id_type=MESH
    )


def greet(row, col, rows_n, cols_n):
    barrier = pltpu.get_barrier_semaphore()
    for k in range(1, cols_n):
        pl.semaphore_signal(barrier, inc=1, device_id=(row, (col + k) % cols_n), device_id_type=MESH)
    for k in range(1, rows_n):
        pl.semaphore_signal(barrier, inc=1, device_id=((row + k) % rows_n, col), device_id_type=MESH)
    pl.semaphore_wait(barrier, cols_n - 1 + rows_n - 1)


def whole_kernel(
    take, slots, late, x_ref, v_ref, e_ref, known_ref, move_ref, straight_ref, turned_ref,
    t_ref, o_ref, chi_ref, buf, rest, e_main, e_rest, e_spread, e_high, e_low, chi_sum, chi_got,
    spread, high, low, w_high, w_low, picked, part_ref, got, last, onward, sums, middle,
    sem, own, send_a, recv_a, send_u, recv_u, send_d, recv_d, send_c, recv_c, send_p, recv_p, send_r, recv_r,
    xsend_a, xrecv_a, xsend_b, xrecv_b, xsend_c, xrecv_c, xsend_d, xrecv_d, xsend_e, xrecv_e, xown,
):
    a_count, b_count, c_count, virtual = v_ref.shape
    rows_n, chunks, cols_n, n, width = t_ref.shape
    levels = rows_n // 2
    row, col = lax.axis_index("row"), lax.axis_index("col")
    level, core = row // 2, row % 2
    twin = row + 1 - 2 * core
    group, lanes = buf.shape[3], buf.shape[4]
    tail = virtual - lanes
    rows = take * b_count
    blocks = a_count // take
    steps = chunks * blocks
    per = lanes // tail
    few = e_ref.shape[0] * e_ref.shape[1]
    pairs = rows_n * cols_n * n
    early = chunks - late
    dims = ((1,), (1,))
    flips = (col + 1 - 2 * (col % 2), (col + 2) % 4)
    far = 3 - col

    def where(step):
        after = step - early * blocks
        is_late = step >= early * blocks
        chunk = jnp.where(is_late, early + lax.rem(jnp.maximum(after, 0), late), step // blocks)
        block = jnp.where(is_late, jnp.maximum(after, 0) // late, lax.rem(step, blocks))
        return chunk, block

    def fetch(step):
        slot = lax.rem(step, slots)
        chunk, block = where(step)
        source = v_ref.at[
            pl.ds(block * take, take), :, pl.ds(pl.multiple_of(chunk * group, group), group), :
        ]
        return (
            pltpu.make_async_copy(source.at[:, :, :, pl.ds(0, lanes)], buf.at[slot], sem.at[slot, 0]),
            pltpu.make_async_copy(source.at[:, :, :, pl.ds(lanes, tail)], rest.at[slot], sem.at[slot, 1]),
        )

    def fetch_few():
        return (
            pltpu.make_async_copy(e_ref.at[:, :, :, pl.ds(0, lanes)], e_main, own.at[chunks]),
            pltpu.make_async_copy(e_ref.at[:, :, :, pl.ds(lanes, tail)], e_rest, own.at[chunks + 1]),
        )

    def keep(c):
        return pltpu.make_async_copy(x_ref.at[col, c], t_ref.at[row, c, col], own.at[c])

    def deal(k, c):
        q = (col + k) % cols_n
        return remote(x_ref.at[q, c], t_ref.at[row, c, col], send_a.at[c, k], recv_a.at[c, k], row, q)

    def dealt(k, c):
        q = (col + cols_n - k) % cols_n
        return remote(x_ref.at[col, c], t_ref.at[row, c, q], send_a.at[c, k], recv_a.at[c, k], row, q)

    def up(k, c):
        at = t_ref.at[jnp.maximum(row - 2 * k, core), c]
        return remote(at, at, send_u.at[c, k], recv_u.at[c, k], jnp.minimum(row + 2, rows_n - 2 + core), col)

    def down(k, c):
        at = t_ref.at[jnp.minimum(row + 2 * k, rows_n - 2 + core), c]
        return remote(at, at, send_d.at[c, k], recv_d.at[c, k], jnp.maximum(row - 2, core), col)

    def came_up(k, c):
        at = t_ref.at[jnp.maximum(row - 2 * k, core), c]
        return remote(at, at, send_u.at[c, k - 1], recv_u.at[c, k - 1], jnp.maximum(row - 2, core), col)

    def came_down(k, c):
        at = t_ref.at[jnp.minimum(row + 2 * k, rows_n - 2 + core), c]
        return remote(at, at, send_d.at[c, k - 1], recv_d.at[c, k - 1], jnp.minimum(row + 2, rows_n - 2 + core), col)

    def share(m, c):
        at = t_ref.at[2 * m + core, c]
        return remote(at, at, send_c.at[c, m], recv_c.at[c, m], twin, col)

    def shared(m, c):
        at = t_ref.at[2 * m + 1 - core, c]
        return remote(at, at, send_c.at[c, m], recv_c.at[c, m], twin, col)

    def open_up(c):
        keep(c).wait()
        for k in range(1, cols_n):
            dealt(k, c).wait_recv()

        @pl.when(level < levels - 1)
        def _():
            up(0, c).start()

        @pl.when(level > 0)
        def _():
            down(0, c).start()

        share(level, c).start()

    def relay(k, c):
        @pl.when(level >= k)
        def _():
            came_up(k, c).wait_recv()

            @pl.when(level < levels - 1)
            def _():
                up(k, c).start()

            share(level - k, c).start()

        @pl.when(level + k <= levels - 1)
        def _():
            came_down(k, c).wait_recv()

            @pl.when(level > 0)
            def _():
                down(k, c).start()

            share(level + k, c).start()

    def settle(c):
        for m in range(levels):
            shared(m, c).wait_recv()

    def plane(k):
        q = (col + k) % cols_n
        return remote(chi_sum, chi_got.at[k], send_p.at[k], recv_p.at[k], row, q)

    def column(k):
        r = (row + k) % rows_n
        return remote(chi_ref.at[row], chi_ref.at[row], send_r.at[k], recv_r.at[k], r, col)

    def columned(k):
        r = (row + rows_n - k) % rows_n
        return remote(chi_ref.at[r], chi_ref.at[r], send_r.at[k], recv_r.at[k], r, col)

    for step in range(slots - 1):
        for copy in fetch(step):
            copy.start()
    for copy in fetch_few():
        copy.start()
    greet(row, col, rows_n, cols_n)
    for c in range(chunks):
        keep(c).start()
        for k in range(1, cols_n):
            deal(k, c).start()
    o_ref[...] = jnp.zeros_like(o_ref)
    chi_sum[...] = jnp.zeros_like(chi_sum)
    for copy in fetch_few():
        copy.wait()
    open_up(0)
    open_up(1)
    for k in range(1, levels):
        relay(k, 0)
    settle(0)

    def lay(main, spread, start, stride, count, high, low):
        lane = lax.broadcasted_iota(jnp.int32, (count, lanes), 1)
        packed = None
        for c in range(group):
            hi, lo = split(main[pl.ds(start + c, count, stride=stride), :])
            high[:, c * lanes : (c + 1) * lanes] = hi
            low[:, c * lanes : (c + 1) * lanes] = lo
            piece = spread[pl.ds(start + c, count, stride=stride), :]
            k = c % per
            packed = piece if k == 0 else jnp.where(lane < tail * k, packed, pltpu.roll(piece, tail * k, 1))
            if k == per - 1:
                at = (group + c // per) * lanes
                hi, lo = split(packed)
                high[:, at : at + lanes] = hi
                low[:, at : at + lanes] = lo

    def pair(k):
        return flips if k < rows_n // 2 else (flips[1], flips[0])

    def scatter(p, k):
        near = pair(k)[0]
        return [
            remote(part_ref.at[p, q, k], got.at[p, k, m], xsend_a.at[p, k, m], xrecv_a.at[p, k, m], row, near)
            for m, q in enumerate((near, far))
        ]

    def pass_on(p, k):
        return remote(onward.at[p, k], last.at[p, k], xsend_b.at[p, k], xrecv_b.at[p, k], row, pair(k)[1])

    def deliver(p, k):
        return remote(sums.at[p, k], straight_ref.at[row, p], xsend_c.at[p, k], xrecv_c.at[p, row], k, col)

    def delivered(p, k):
        return remote(sums.at[p, k], straight_ref.at[k, p], xsend_c.at[p, k], xrecv_c.at[p, k], k, col)

    def deliver_own(p, k):
        return pltpu.make_async_copy(sums.at[p, k], straight_ref.at[row, p], xown.at[p, 0])

    def cross(p, k):
        return remote(
            sums.at[p, k], middle.at[p, k % 2, col], xsend_d.at[p, k], xrecv_d.at[p, k % 2, col], row, k // 2
        )

    def crossed(p, m, q):
        return remote(sums.at[p, m], middle.at[p, m, q], xsend_d.at[p, m], xrecv_d.at[p, m, q], row, q)

    def cross_own(p, k):
        return pltpu.make_async_copy(sums.at[p, k], middle.at[p, k % 2, col], xown.at[p, 1 + k % 2])

    def fan(p, m, q, h):
        return remote(
            middle.at[p, m, q, h], turned_ref.at[row, p, m],
            xsend_e.at[p, m, q, h], xrecv_e.at[p, row, m], 2 * q + h, col,
        )

    def fanned(p, m, k):
        return remote(
            middle.at[p, m, k // 2, k % 2], turned_ref.at[k, p, m],
            xsend_e.at[p, m, k // 2, k % 2], xrecv_e.at[p, k, m], k, col,
        )

    def fan_own(p, m, q, h):
        return pltpu.make_async_copy(middle.at[p, m, q, h], turned_ref.at[row, p, m], xown.at[p, 3 + m])

    order = [k for m in range(rows_n // 2) for k in (m, rows_n // 2 + m)]

    def launch(p):
        turned = o_ref[pl.ds(pl.multiple_of(p * rows, rows), rows), :].T
        for r in range(rows_n):
            for q in range(cols_n):
                for h in range(2):
                    at = (r * cols_n + q) * n + h * n // 2
                    part_ref[p, q, r, h] = turned[at : at + n // 2, :]
        for k in order:
            for copy in scatter(p, k):
                copy.start()

    def first(p):
        for k in order:
            for copy in scatter(p, k):
                copy.wait_recv()
            onward[p, k] = part_ref[p, pair(k)[1], k] + got[p, k, 1]
            sums[p, k] = part_ref[p, col, k] + got[p, k, 0]
            pass_on(p, k).start()

    def second(p):
        for k in order:
            pass_on(p, k).wait_recv()
            sums[p, k] = sums[p, k] + last[p, k]

            @pl.when(col != k // 2)
            def _():
                cross(p, k).start()

            @pl.when(col == k // 2)
            def _():
                cross_own(p, k).start()

            @pl.when(row != k)
            def _():
                deliver(p, k).start()

            @pl.when(row == k)
            def _():
                deliver_own(p, k).start()

    def third(p):
        for k in order:
            m = k % 2

            @pl.when(col == k // 2)
            def _():
                cross_own(p, k).wait()
                for q in range(cols_n):
                    @pl.when(col != q)
                    def _():
                        crossed(p, m, q).wait_recv()

                    for h in range(2):
                        @pl.when(row != 2 * q + h)
                        def _():
                            fan(p, m, q, h).start()

                        @pl.when(row == 2 * q + h)
                        def _():
                            fan_own(p, m, q, h).start()

    def drain(p):
        for k in order:
            for copy in scatter(p, k):
                copy.wait_send()
            pass_on(p, k).wait_send()

            @pl.when(row != k)
            def _():
                deliver(p, k).wait_send()
                delivered(p, k).wait_recv()
                for m in range(2):
                    fan(p, m, k // 2, k % 2).wait_send()
                    fanned(p, m, k).wait_recv()

            @pl.when(row == k)
            def _():
                deliver_own(p, k).wait()
                for m in range(2):
                    fan_own(p, m, k // 2, k % 2).wait()

            @pl.when(col != k // 2)
            def _():
                cross(p, k).wait_send()

    def triple(high, low, w):
        return (
            product(high[...], w_high[w], dims)
            + product(low[...], w_high[w], dims)
            + product(high[...], w_low[w], dims)
        )

    e_spread[:, pl.ds(0, tail)] = e_rest.reshape(few * c_count, tail)[...]
    tall = -(-a_count // 16) * 16
    spot = row * a_count + lax.broadcasted_iota(jnp.int32, (tall, lanes), 0)
    lane = lax.broadcasted_iota(jnp.int32, (tall, lanes), 1)
    choose = jnp.where(spot == lane, 1.0, 0.0).astype(BF16)
    later = []
    for k in range(per):
        hit = (spot - lanes == lane - k * tail) & (lane >= k * tail) & (lane < (k + 1) * tail)
        later.append(jnp.where(hit, 1.0, 0.0).astype(BF16))

    def prepare(chunk, w):
        for r in range(rows_n):
            for q in range(cols_n):
                at = (r * cols_n + q) * n
                hi, lo = split(t_ref[r, chunk, q])
                w_high[w, at : at + n, :] = hi
                w_low[w, at : at + n, :] = lo
        for c in range(group):
            at = (group + c // per) * lanes
            total = None
            for ref in (w_high, w_low):
                value = product(choose, ref[w, :, c * lanes : (c + 1) * lanes], dims)
                value += product(later[c % per], ref[w, :, at : at + lanes], dims)
                total = value if total is None else total + value
            for half in range(pairs // lanes):
                picked[half, pl.ds(chunk * group + c, a_count, stride=c_count), :] = total[
                    :a_count, half * lanes : (half + 1) * lanes
                ]
        lay(e_main.reshape(few * c_count, lanes), e_spread, chunk * group, c_count, few, e_high, e_low)
        chi_sum[...] += triple(e_high, e_low, w)

    def multiply(step, block, w):
        slot = lax.rem(step, slots)
        for copy in fetch(step):
            copy.wait()

        @pl.when(step + slots - 1 < steps)
        def _():
            for copy in fetch(step + slots - 1):
                copy.start()

        spread[:, pl.ds(0, tail)] = rest.at[slot].reshape(rows * group, tail)[...]
        lay(buf.at[slot].reshape(rows * group, lanes), spread, 0, group, rows, high, low)
        o_ref[pl.ds(pl.multiple_of(block * rows, rows), rows), :] += triple(high, low, w)

    def opening(step, _):
        chunk, block = step // blocks, lax.rem(step, blocks)
        count = early * blocks
        events = (chunks - 1) * (levels - 1)
        event = (step * events + count - 1) // count
        ahead = 1 + event // (levels - 1)

        @pl.when((event * count // events == step) & (event < events))
        def _():
            for k in range(1, levels):
                @pl.when(lax.rem(event, levels - 1) == k - 1)
                def _():
                    relay(k, ahead)

            @pl.when((lax.rem(event, levels - 1) == 0) & (ahead + 1 < chunks))
            def _():
                open_up(ahead + 1)

        @pl.when(block == 0)
        def _():
            prepare(chunk, 0)

        multiply(step, block, 0)

        @pl.when((block == blocks - 1) & (chunk + 1 < early))
        def _():
            settle(chunk + 1)

        return 0

    lax.fori_loop(0, early * blocks, opening, 0)
    for w in range(late):
        settle(early + w)
        prepare(early + w, w)
    for k in range(1, cols_n):
        plane(k).start()

    def hole():
        for k in range(1, rows_n):
            columned(k).wait_recv()
        turn_high = turn_low = None
        for r in range(rows_n):
            at = slice(r * few, (r + 1) * few)
            hi, lo = split(chi_ref[r] + known_ref[at, :])
            turn = move_ref[:, at]
            hi = product(turn, hi, ((1,), (0,)))
            lo = product(turn, lo, ((1,), (0,)))
            turn_high = hi if turn_high is None else turn_high + hi
            turn_low = lo if turn_low is None else turn_low + lo
        mix_high, mix_low = turn_high.astype(BF16), turn_low.astype(BF16)
        total = None
        for half in range(pairs // lanes):
            hi, lo = split(picked[half])
            at = slice(half * lanes, (half + 1) * lanes)
            value = (
                product(hi, mix_high[at, :], ((1,), (0,)))
                + product(lo, mix_high[at, :], ((1,), (0,)))
                + product(hi, mix_low[at, :], ((1,), (0,)))
            )
            total = value if total is None else total + value
        for a in range(a_count):
            at = pl.ds(pl.multiple_of(a * b_count + col * c_count, 8), c_count)
            o_ref[at, :] += total[a * c_count : (a + 1) * c_count, :]

    def closing(block, _):
        def inner(w, _):
            multiply(early * blocks + block * late + w, block, w)

            @pl.when((block == 0) & (w == 0))
            def _():
                total = chi_sum[...]
                for k in range(1, cols_n):
                    plane(k).wait_recv()
                    total = total + chi_got[k]
                chi_ref[row] = total
                for k in range(1, rows_n):
                    column(k).start()

            @pl.when((w == 0) & (block >= 1))
            def _():
                first(block - 1)

            return 0

        lax.fori_loop(0, late, inner, 0)

        @pl.when(block == 0)
        def _():
            hole()

        launch(block)

        @pl.when(block >= 1)
        def _():
            second(block - 1)

        @pl.when(block >= 2)
        def _():
            third(block - 2)

        return 0

    lax.fori_loop(0, blocks, closing, 0)
    third(blocks - 2)
    first(blocks - 1)
    second(blocks - 1)
    third(blocks - 1)
    lax.fori_loop(0, blocks, lambda p, _: (drain(p), 0)[1], 0)
    for k in range(1, cols_n):
        plane(k).wait_send()
    for k in range(1, rows_n):
        column(k).wait_send()
    for c in range(chunks):
        for k in range(1, cols_n):
            deal(k, c).wait_send()
        for m in range(levels):
            share(m, c).wait_send()
        for k in range(levels - 1):
            @pl.when((level >= k) & (level < levels - 1))
            def _():
                up(k, c).wait_send()

            @pl.when((level + k <= levels - 1) & (level > 0))
            def _():
                down(k, c).wait_send()


def whole(x, v, e, known, move, rows_n, take, slots, late):
    a_count, b_count, c_count, virtual = v.shape
    cols_n, chunks, n, width = x.shape
    pairs = rows_n * cols_n * n
    group, lanes = c_count // chunks, 128
    tail = virtual - lanes
    rows = take * b_count
    blocks = a_count // take
    few = e.shape[0] * e.shape[1]
    levels = rows_n // 2
    block = (2, n // 2, rows)
    dma = pltpu.SemaphoreType.DMA
    vmem = pl.BlockSpec(memory_space=pltpu.VMEM)
    hbm = pl.BlockSpec(memory_space=pl.ANY)
    return pl.pallas_call(
        functools.partial(whole_kernel, take, slots, late),
        out_shape=[jax.ShapeDtypeStruct((rows_n, blocks) + block, F32)] * 2,
        in_specs=[vmem, hbm, hbm, vmem, vmem],
        out_specs=[vmem] * 2,
        scratch_shapes=[
            pltpu.VMEM((rows_n, chunks, cols_n, n, width), F32),
            pltpu.VMEM((a_count * b_count, pairs), F32),
            pltpu.VMEM((rows_n, few, pairs), F32),
            pltpu.VMEM((slots, take, b_count, group, lanes), F32),
            pltpu.VMEM((slots, take, b_count, group, tail), F32),
            pltpu.VMEM(e.shape[:3] + (lanes,), F32),
            pltpu.VMEM(e.shape[:3] + (tail,), F32),
            pltpu.VMEM((few * c_count, lanes), F32),
            pltpu.VMEM((few, width), BF16),
            pltpu.VMEM((few, width), BF16),
            pltpu.VMEM((few, pairs), F32),
            pltpu.VMEM((cols_n, few, pairs), F32),
            pltpu.VMEM((rows * group, lanes), F32),
            pltpu.VMEM((rows, width), BF16),
            pltpu.VMEM((rows, width), BF16),
            pltpu.VMEM((late, pairs, width), BF16),
            pltpu.VMEM((late, pairs, width), BF16),
            pltpu.VMEM((pairs // lanes, a_count * c_count, lanes), F32),
            pltpu.VMEM((blocks, cols_n, rows_n) + block, F32),
            pltpu.VMEM((blocks, rows_n, 2) + block, F32),
            pltpu.VMEM((blocks, rows_n) + block, F32),
            pltpu.VMEM((blocks, rows_n) + block, F32),
            pltpu.VMEM((blocks, rows_n) + block, F32),
            pltpu.VMEM((blocks, 2, cols_n) + block, F32),
            dma((slots, 2)), dma((chunks + 2,)),
            dma((chunks, cols_n)), dma((chunks, cols_n)),
            dma((chunks, levels)), dma((chunks, levels)),
            dma((chunks, levels)), dma((chunks, levels)),
            dma((chunks, levels)), dma((chunks, levels)),
            dma((cols_n,)), dma((cols_n,)),
            dma((rows_n,)), dma((rows_n,)),
            dma((blocks, rows_n, 2)), dma((blocks, rows_n, 2)),
            dma((blocks, rows_n)), dma((blocks, rows_n)),
            dma((blocks, rows_n)), dma((blocks, rows_n)),
            dma((blocks, rows_n)), dma((blocks, 2, cols_n)),
            dma((blocks, 2, cols_n, 2)), dma((blocks, rows_n, 2)),
            dma((blocks, 5)),
        ],
        compiler_params=pltpu.CompilerParams(
            collective_id=0, has_side_effects=True, vmem_limit_bytes=62 << 20
        ),
    )(x, v, e, known, move)


def fast(amplitudes, vvvv, hole_ints, exchange_ints, fock_occ, fock_vir, eps_occ, eps_vir):
    high = lax.Precision.HIGH
    rows_n = lax.axis_size("row")
    cols_n = lax.axis_size("col")
    row = lax.axis_index("row")
    col = lax.axis_index("col")
    first, second, virtual = amplitudes.shape[:3]
    occupied = fock_occ.shape[0]
    pairs = occupied * occupied
    a_count, c_count = vvvv.shape[0], vvvv.shape[2]
    group, lanes = 8, 128
    tail = virtual - lanes
    chunks = c_count // group
    n = first * second

    half = second // 2
    x = amplitudes.reshape(first, 2, half, virtual, virtual).transpose(1, 0, 2, 3, 4)
    x = x.reshape(n, cols_n, chunks, group, virtual)
    x = jnp.concatenate(
        [
            x[..., :lanes].reshape(n, cols_n, chunks, group * lanes),
            x[..., lanes:].reshape(n, cols_n, chunks, group * tail),
        ],
        axis=-1,
    ).transpose(1, 2, 0, 3)
    delta = jnp.eye(occupied, dtype=fock_occ.dtype)
    known = hole_ints - delta[:, None, :, None] * fock_occ[None, :, None, :]
    highest = lax.Precision.HIGHEST
    one, two = np.divmod(np.arange(pairs), occupied)

    def place(i, j):
        inner = (j % second) // half * (first * half) + (i % first) * half + j % half
        return ((i // first) * cols_n + j // second) * n + inner

    spots = np.arange(pairs)
    turn = jnp.asarray((place(one, two)[:, None] == spots[None, :]).astype(np.float32))
    move = jnp.asarray((spots[:, None] == place(two, one)[None, :]).astype(np.float32), BF16)

    known = jnp.dot(known.reshape(pairs, pairs), turn, precision=highest)


    straight, turned = whole(x, vvvv, exchange_ints, known, move, rows_n, 4, 3, 2)
    blocks = a_count // 4
    straight = straight.reshape(rows_n, blocks, 2, first, half, 4, virtual)
    straight = straight.transpose(3, 2, 4, 0, 1, 5, 6).reshape(first, second, virtual, virtual)
    turned = turned.reshape(rows_n, blocks, 2, half, first, 4, virtual)
    turned = turned.transpose(4, 2, 3, 6, 0, 1, 5).reshape(first, second, virtual, virtual)
    return close(straight + turned, amplitudes, fock_vir, eps_occ, eps_vir)


def on_device(amplitudes, vvvv, *rest):
    virtual, b_count, c_count = amplitudes.shape[2], vvvv.shape[1], vvvv.shape[2]
    tail = virtual - 128
    fits = (
        virtual > 128
        and 128 % tail == 0
        and c_count % 8 == 0
        and c_count >= 24
        and (c_count // 8 - 2) * (vvvv.shape[0] // 4) >= (c_count // 8 - 1) * (lax.axis_size("row") // 2 - 1)
        and (8 * tail) % 128 == 0
        and vvvv.shape[0] % 4 == 0
        and (4 * b_count) % 128 == 0
        and (amplitudes.shape[0] * amplitudes.shape[1]) % 8 == 0
        and amplitudes.shape[1] == 2 * amplitudes.shape[0]
        and lax.axis_size("row") == 2 * lax.axis_size("col")
        and lax.axis_size("col") == 4
    )
    return (fast if fits else plain)(amplitudes, vvvv, *rest)


def solution(mesh):
    in_specs = (
        P("row", "col", None, None),
        P("row", None, "col", None),
        P(),
        P("row", None, "col", None),
        P(),
        P(),
        P(),
        P(),
    )
    out_specs = P("row", "col", None, None)
    return jax.shard_map(
        on_device, mesh=mesh, in_specs=in_specs, out_specs=out_specs, check_vma=False
    )
```
